32 devices in a mesh: replica: 8 (over z, core), fsdp: 4 (over y, x).
Axes of the slice: x: 2, y: 2, z: 4, core: 2. Of those that a mesh axis runs over, the one named last changes fastest.
Arguments:
- weights: bfloat16 [4096, 14336], P(None, 'fsdp'), may hold values from -6 to 6
- head_vector: float32 [14336], P('fsdp'), may hold values from -6 to 6
- momentum: float32 [4096, 14336], P('replica', 'fsdp'), may hold values from -4 to 4
- batches: bfloat16 [1, 2048, 4096], P(None, ('replica', 'fsdp')), may hold values from -6 to 6
- pair_index: int32 [1, 1024, 2], P(None, 'replica'), may hold values from 0 to 255, as said below
- eval_rows: bfloat16 [256, 4096], P(('replica', 'fsdp')), may hold values from -6 to 6
Outputs:
- momentum_out: float32 [4096, 14336], P('replica', 'fsdp')
- eval_rewards: float32 [256], P(('replica', 'fsdp'))
The draws below stay inside these ranges and needn't reach their ends.
Inputs may be any that keep to these rules, and one draw needn't show every extreme that they name: `pair_index`: each pair names two different rows among its replica's 256 rows of that step; the first is the preferred one.
All inputs are finite; a program needn't handle non-finite values.
Results may differ from the reference program's by a relative error of at most 0.0038.
Values may be sent and summed in bfloat16 or wider, within the bound.
No kernel may reach another device: no remote copies, remote signals or barrier semaphores. Data moves between devices by JAX's collectives and lax.ppermute only.
A program may use at most 320 MiB of HBM per device.

```python
import jax
import jax.numpy as jnp
from jax import lax

D = 4096
FF = 14336
BLOCK = 128
STEPS = 1
REP_TOKENS = 256
TOKENS_ALL = 2048
PAIRS_ALL = 1024
EVAL_ALL = 256
N_REPLICA = 8


def draw_pair_index(key, part):
    first_key, second_key = jax.random.split(jax.random.fold_in(key, 17))
    chosen = jax.random.randint(first_key, (STEPS, PAIRS_ALL), 0, REP_TOKENS, dtype=jnp.int32)
    offset = jax.random.randint(second_key, (STEPS, PAIRS_ALL), 1, REP_TOKENS, dtype=jnp.int32)
    return jnp.stack([chosen, (chosen + offset) % REP_TOKENS], axis=-1)


def block_levels(stream_key, extent, pieces, low, high):
    def one(position, blocks):
        draws = jax.random.uniform(jax.random.fold_in(jax.random.fold_in(stream_key, 6), position), (blocks,), jnp.float32, low / len(pieces), high / len(pieces))
        return jnp.repeat(jnp.exp(draws), extent[position] // blocks).reshape((-1,) + (1,) * (len(extent) - position - 1))

    level = one(*pieces[0])
    for cut in pieces[1:]:
        level = level * one(*cut)
    return level


def noise(rng, dims, width, bound, shards=(), held_as=jnp.bfloat16):
    gain = block_levels(rng, dims, shards, -0.22, 0.18) if shards else 1.0
    result = jax.random.normal(rng, dims, jnp.float32) * width * gain
    return jnp.minimum(jnp.maximum(result, -bound), bound).astype(held_as)


def setup_inputs(seed: int = 0) -> dict:
    key_of = jax.random.split(jax.random.key(seed), 7)
    return {
        "weights": noise(key_of[0], (D, FF), 1.0, 6.0, ((1, 4),)),
        "head_vector": noise(key_of[1], (FF,), 1.0, 6.0, ((0, 4),), jnp.float32),
        "momentum": noise(key_of[2], (D, FF), 0.3, 4.0, ((0, 8), (1, 4)), jnp.float32),
        "batches": noise(key_of[3], (STEPS, TOKENS_ALL, D), 1.0, 6.0, ((1, 32),)),
        "pair_index": draw_pair_index(jax.random.fold_in(key_of[6], 71), 0),
        "eval_rows": noise(key_of[5], (EVAL_ALL, D), 1.0, 6.0, ((0, 32),)),
    }


inner_rate = 300.0
outer_rate = 0.7
outer_decay = 0.9
code_top = 448.0
epsilon = 1e-06

def forward(inputs, current, head_vector):
    hidden = jnp.dot(inputs, current, preferred_element_type=jnp.float32) * D ** (-0.5)
    squash = jax.nn.sigmoid(hidden)
    rewards = jnp.dot(hidden * squash, head_vector, precision=lax.Precision.HIGHEST) * FF ** (-0.5)
    return (hidden, squash, rewards)

def weight_grad(inputs, pair_local, current, head_vector):
    hidden, squash, rewards = forward(inputs, current, head_vector)
    chosen = pair_local[:, 0]
    rejected = pair_local[:, 1]
    pair_weight = jax.nn.sigmoid(rewards[rejected] - rewards[chosen])
    reward_grad = jnp.zeros_like(rewards).at[rejected].add(pair_weight).at[chosen].add(-pair_weight)
    head_scaled = head_vector * FF ** (-0.5)
    hidden_grad = (reward_grad[:, None] * head_scaled[None, :] * squash * (1.0 + hidden * (1.0 - squash))).astype(jnp.bfloat16)
    return lax.dot_general(inputs, hidden_grad, (((0,), (0,)), ((), ())), preferred_element_type=jnp.float32) * D ** (-0.5)

def quantize(matrix):
    blocks = matrix.reshape(matrix.shape[0] // BLOCK, BLOCK, matrix.shape[1])
    largest = lax.optimization_barrier(jnp.max(jnp.abs(blocks), axis=1))
    block_scale = ((largest + epsilon) / code_top).astype(jnp.bfloat16)
    coded = (blocks / block_scale.astype(jnp.float32)[:, None, :]).astype(jnp.bfloat16)
    return (coded.reshape(matrix.shape), block_scale)

def decode(coded, block_scale):
    blocks = coded.reshape(block_scale.shape[0], -1, coded.shape[1]).astype(jnp.float32)
    return (blocks * block_scale.astype(jnp.float32)[:, None, :]).reshape(coded.shape)

def local_delta(weights, head_vector, inputs_steps, pair_steps):
    accumulated = jnp.zeros(weights.shape, jnp.float32)
    current = weights
    for inner_step in range(STEPS):
        accumulated = accumulated + weight_grad(inputs_steps[inner_step], pair_steps[inner_step], current, head_vector)
        current = (weights.astype(jnp.float32) - inner_rate * accumulated).astype(jnp.bfloat16)
    return inner_rate * accumulated

def reference(weights, head_vector, momentum, batches, pair_index, eval_rows):
    replica_rows = batches.shape[1] // N_REPLICA
    replica_pairs = pair_index.shape[1] // N_REPLICA

    def one_replica(running, replica_index):
        inputs_steps = lax.dynamic_slice_in_dim(batches, replica_index * replica_rows, replica_rows, 1)
        pair_steps = lax.dynamic_slice_in_dim(pair_index, replica_index * replica_pairs, replica_pairs, 1)
        coded, block_scale = quantize(local_delta(weights, head_vector, inputs_steps, pair_steps))
        return (running + decode(coded, block_scale), None)
    scanned = lax.scan(one_replica, jnp.zeros(weights.shape, jnp.float32), jnp.arange(N_REPLICA, dtype=jnp.int32))
    pseudo = scanned[0] / N_REPLICA
    momentum_out = outer_decay * momentum + pseudo
    update = outer_rate * (pseudo + outer_decay * momentum_out)
    coded, block_scale = quantize(update)
    new_weights = (weights.astype(jnp.float32) - decode(coded, block_scale)).astype(jnp.bfloat16)
    eval_rewards = forward(eval_rows, new_weights, head_vector)[2]
    return (momentum_out, eval_rewards)
```

```python
import functools

import jax
import jax.numpy as jnp
from jax import lax
from jax.experimental import pallas as pl
from jax.experimental.pallas import tpu as pltpu
from jax.sharding import Mesh
from jax.sharding import PartitionSpec as P

BLOCK = 128

inner_rate = 300.0
outer_rate = 0.7
outer_decay = 0.9
code_top = 448.0
epsilon = 1e-06

f32 = jnp.float32
bf16 = jnp.bfloat16


def tile_of(extent, top):
    tile = top
    while extent % tile:
        tile //= 2
    return tile


def whole(shape):
    return pl.BlockSpec(shape, lambda *_: (0,) * len(shape))


def params(mib=48):
    return pltpu.CompilerParams(
        dimension_semantics=("arbitrary",), vmem_limit_bytes=mib << 20
    )


def forward_kernel(places, scale, own_rows, where, *refs):
    blocks = refs[: len(places)]
    w, head, hidden, partial, mine_t, other_t, rows, sums = refs[len(places) :]

    @pl.when(pl.program_id(0) == 0)
    def _():
        for (start, size), block in zip(places, blocks):
            rows[start : start + size, :] = block[...]
        sums[...] = jnp.zeros_like(sums)
        for place, out in ((0, mine_t), (1, other_t)):
            begin = pl.multiple_of(where[place] * own_rows, 128)
            out[...] = rows[:, pl.ds(begin, own_rows)].T

    value = jnp.dot(rows[...], w[...], preferred_element_type=f32) * scale
    hidden[...] = value
    term = value * jax.nn.sigmoid(value) * head[...]
    total = sums[...]
    for lane in range(0, term.shape[1], 128):
        total = total + term[:, lane : lane + 128]
    sums[...] = total

    @pl.when(pl.program_id(0) == pl.num_programs(0) - 1)
    def _():
        column = jnp.sum(sums[...], axis=1, keepdims=True)
        partial[...] = jnp.broadcast_to(column, sums.shape).T[0:1, :]


def forward_call(where, blocks, places, weights, head, own_rows):
    depth, columns = weights.shape
    count = sum(size for _, size in places)
    tile = tile_of(columns, 512)
    return pl.pallas_call(
        functools.partial(forward_kernel, places, depth ** (-0.5), own_rows),
        out_shape=(
            jax.ShapeDtypeStruct((count, columns), f32),
            jax.ShapeDtypeStruct((1, count), f32),
            jax.ShapeDtypeStruct((own_rows, count), bf16),
            jax.ShapeDtypeStruct((own_rows, count), bf16),
        ),
        grid_spec=pltpu.PrefetchScalarGridSpec(
            num_scalar_prefetch=1,
            grid=(columns // tile,),
            in_specs=[whole(block.shape) for block in blocks]
            + [
                pl.BlockSpec((depth, tile), lambda j, *_: (0, j)),
                pl.BlockSpec((1, tile), lambda j, *_: (0, j)),
            ],
            out_specs=[
                pl.BlockSpec((count, tile), lambda j, *_: (0, j)),
                whole((1, count)),
                whole((own_rows, count)),
                whole((own_rows, count)),
            ],
            scratch_shapes=[
                pltpu.VMEM((count, depth), bf16),
                pltpu.VMEM((count, 128), f32),
            ],
        ),
        compiler_params=params(),
        cost_estimate=pl.CostEstimate(
            flops=2 * count * depth * columns,
            bytes_accessed=2 * depth * columns + 4 * count * columns,
            transcendentals=count * columns,
        ),
    )(where, *blocks, weights, head)


def grad_kernel(group, scale, pairs, *refs):
    partials = refs[:group]
    hidden, head, out, reward_grad = refs[group:]

    @pl.when(pl.program_id(0) == 0)
    def _():
        n_pairs = pairs.shape[1]
        rows = reward_grad.shape[0]
        size = rows // group
        rewards = jnp.zeros((rows, n_pairs), f32)
        for k, partial in enumerate(partials):
            column = jnp.broadcast_to(partial[...], (n_pairs, rows)).T
            rewards = rewards + jnp.concatenate(
                [column[(j ^ k) * size : (j ^ k) * size + size] for j in range(group)], axis=0
            )
        rewards = rewards * scale
        position = lax.broadcasted_iota(jnp.int32, (rows, n_pairs), 0)
        table = (position == pairs[1:2, :]).astype(f32) - (position == pairs[0:1, :]).astype(f32)
        gap = jnp.sum(table * rewards, axis=0, keepdims=True)
        pair_weight = jax.nn.sigmoid(gap)
        column = jnp.sum(table * pair_weight, axis=1, keepdims=True)
        reward_grad[...] = jnp.broadcast_to(column, reward_grad.shape)

    value = hidden[...]
    squash = jax.nn.sigmoid(value)
    head_scaled = head[...] * scale
    out[...] = (
        reward_grad[:, 0:1] * head_scaled * squash * (1.0 + value * (1.0 - squash))
    ).astype(bf16)


def grad_call(pairs, partials, hidden, head, hidden_units):
    rows, columns = hidden.shape
    tile = tile_of(columns, 512)
    return pl.pallas_call(
        functools.partial(grad_kernel, len(partials), hidden_units ** (-0.5)),
        out_shape=jax.ShapeDtypeStruct((rows, columns), bf16),
        grid=(columns // tile,),
        in_specs=[whole(pairs.shape)]
        + [whole(partial.shape) for partial in partials]
        + [
            pl.BlockSpec((rows, tile), lambda j: (0, j)),
            pl.BlockSpec((1, tile), lambda j: (0, j)),
        ],
        out_specs=pl.BlockSpec((rows, tile), lambda j: (0, j)),
        scratch_shapes=[pltpu.VMEM((rows, 128), f32)],
        compiler_params=params(),
        cost_estimate=pl.CostEstimate(
            flops=10 * rows * columns,
            bytes_accessed=6 * rows * columns,
            transcendentals=rows * columns,
        ),
    )(pairs, *partials, hidden, head)


def coded_sum(x_t, grad, factor, total):
    raw = jnp.dot(x_t, grad, preferred_element_type=f32)
    parts = []
    for start in range(0, raw.shape[0], BLOCK):
        block = raw[start : start + BLOCK]
        largest = jnp.max(jnp.abs(block), axis=0, keepdims=True) * factor
        scale = ((largest + epsilon) / code_top).astype(bf16).astype(f32)
        coded = (block * (factor / scale)).astype(bf16)
        parts.append(coded.astype(f32) * scale)
    decoded = jnp.concatenate(parts, axis=0)
    return decoded if total is None else total + decoded


def delta_kernel(first, factor, *refs):
    total = None
    if not first:
        total = refs[0][...]
        refs = refs[1:]
    mine_t, mine_grad, other_t, other_grad, out = refs
    total = coded_sum(mine_t[...], mine_grad[...], factor, total)
    out[...] = coded_sum(other_t[...], other_grad[...], factor, total)


def delta_call(total, mine_t, mine_grad, other_t, other_grad, factor):
    own_rows, rows = mine_t.shape
    columns = mine_grad.shape[1]
    tile = tile_of(columns, 256)
    first = total is None
    total_spec = pl.BlockSpec((own_rows, tile), lambda j: (0, j))
    grad_spec = pl.BlockSpec((rows, tile), lambda j: (0, j))
    return pl.pallas_call(
        functools.partial(delta_kernel, first, factor),
        out_shape=jax.ShapeDtypeStruct((own_rows, columns), f32),
        grid=(columns // tile,),
        in_specs=([] if first else [total_spec])
        + [whole((own_rows, rows)), grad_spec, whole((own_rows, rows)), grad_spec],
        out_specs=total_spec,
        input_output_aliases={} if first else {0: 0},
        compiler_params=params(),
        cost_estimate=pl.CostEstimate(
            flops=4 * own_rows * rows * columns,
            bytes_accessed=8 * own_rows * columns + 4 * rows * columns,
            transcendentals=0,
        ),
    )(*(() if first else (total,)), mine_t, mine_grad, other_t, other_grad)


def settle_kernel(chained, factor, replicas, order, where, *refs):
    if chained:
        refs = refs[1:]
    (total, mine_t, mine_grad, other_t, other_grad, momentum, w, rows) = refs[:8]
    momentum_out, near, far, sorted_rows, new_w = refs[8:]
    slots = order.shape[0]
    size = rows.shape[0] // slots

    @pl.when(pl.program_id(0) == 0)
    def _():
        for slot in range(slots):
            begin = pl.multiple_of(order[slot] * size, size)
            sorted_rows[slot * size : (slot + 1) * size, :] = rows[pl.ds(begin, size), :]

    summed = coded_sum(mine_t[...], mine_grad[...], factor, total[...])
    summed = coded_sum(other_t[...], other_grad[...], factor, summed)
    for start in range(0, summed.shape[0], BLOCK):
        part = slice(start, start + BLOCK)
        pseudo = summed[part] / replicas
        moved = outer_decay * momentum[part, :] + pseudo
        momentum_out[part, :] = moved
        update = outer_rate * (pseudo + outer_decay * moved)
        largest = jnp.max(jnp.abs(update), axis=0, keepdims=True)
        scale = ((largest + epsilon) / code_top).astype(bf16).astype(f32)
        coded = (update * (1.0 / scale)).astype(bf16)
        new_w[part, :] = (w[part, :].astype(f32) - coded.astype(f32) * scale).astype(bf16)
    value = jnp.dot(sorted_rows[...], new_w[...], preferred_element_type=f32)
    half = value.shape[0] // 2
    near[...] = value[:half]
    far[...] = value[half:]


def settle_call(
    part, parts, chain, order, where, total, mine_t, mine_grad, other_t, other_grad,
    momentum, weights, rows, factor, replicas,
):
    own_rows, depth = mine_t.shape
    columns = mine_grad.shape[1]
    tile = tile_of(columns // parts, 256)
    steps = columns // parts // tile
    base = part * steps
    chained = chain is not None
    down = lambda j, *_: (0, base + j)
    out_rows = rows.shape[0] // 2
    return pl.pallas_call(
        functools.partial(settle_kernel, chained, factor, replicas),
        out_shape=(
            jax.ShapeDtypeStruct((own_rows, columns), f32),
            jax.ShapeDtypeStruct((out_rows, columns // parts), f32),
            jax.ShapeDtypeStruct((out_rows, columns // parts), f32),
        ),
        grid_spec=pltpu.PrefetchScalarGridSpec(
            num_scalar_prefetch=2,
            grid=(steps,),
            in_specs=([pl.BlockSpec(memory_space=pl.ANY)] if chained else [])
            + [
                pl.BlockSpec((own_rows, tile), down),
                whole((own_rows, depth)),
                pl.BlockSpec((depth, tile), down),
                whole((own_rows, depth)),
                pl.BlockSpec((depth, tile), down),
                pl.BlockSpec((own_rows, tile), down),
                pl.BlockSpec((own_rows, tile), lambda j, order, where: (where[0], base + j)),
                whole(rows.shape),
            ],
            out_specs=[
                pl.BlockSpec((own_rows, tile), down),
                pl.BlockSpec((out_rows, tile), lambda j, *_: (0, j)),
                pl.BlockSpec((out_rows, tile), lambda j, *_: (0, j)),
            ],
            scratch_shapes=[
                pltpu.VMEM(rows.shape, bf16),
                pltpu.VMEM((own_rows, tile), bf16),
            ],
        ),
        input_output_aliases={2: 0} if chained else {},
        compiler_params=params(),
        cost_estimate=pl.CostEstimate(
            flops=(4 * own_rows * depth + 2 * own_rows * rows.shape[0]) * columns // parts,
            bytes_accessed=(14 * own_rows + 4 * depth + 4 * rows.shape[0]) * columns // parts,
            transcendentals=0,
        ),
    )(
        order, where, *((chain,) if chained else ()), total, mine_t, mine_grad,
        other_t, other_grad, momentum, weights, rows,
    )


def shards(weights, head_vector, momentum, batches, pair_index, eval_rows):
    ring, group = lax.axis_size("ring"), lax.axis_size("fsdp")
    replicas = 2 * ring
    depth, columns = weights.shape
    hidden_units = columns * group
    own_rows = momentum.shape[0]
    block = batches.shape[1]
    at_ring, at_core, at_fsdp = (lax.axis_index(name) for name in ("ring", "core", "fsdp"))
    path = list(range(0, 1)) + list(range(1, ring, 2)) + list(range(2, ring, 2))[::-1]
    spot = [path.index(chip) for chip in range(ring)]
    onward = [(path[i], path[(i + 1) % ring]) for i in range(ring)]

    def along(value):
        return lax.ppermute(value, "ring", onward)

    def across(value, k):
        return lax.ppermute(value, "fsdp", [(i, i ^ k) for i in range(group)])

    def swap(value):
        return lax.ppermute(value, "core", [(0, 1), (1, 0)])

    replica = at_ring * 2 + at_core
    where = jnp.stack([replica, at_ring * 2 + 1 - at_core]).astype(jnp.int32)
    head = head_vector.reshape(1, columns)

    pairs = pair_index[0].T
    pairs = ((pairs // block) ^ at_fsdp) * block + pairs % block

    own = batches[0]
    if group == 4:
        half = block // 2
        places = [(0, block), (block, block), (2 * block, block), (3 * block, half), (3 * block + half, half)]
    else:
        places = [(k * block, block) for k in range(group)]

    factor = inner_rate * depth ** (-0.5)
    total = None
    held = None
    for step in range(ring):
        if step:
            own, pairs = along(own), along(pairs)
        if group == 4:
            one, two = across(own, 1), across(own, 2)
            blocks = [own, one, two, across(one[:half], 2), across(two[half:], 1)]
        else:
            blocks = [own] + [across(own, k) for k in range(1, group)]
        hidden, partial, mine_t, other_t = forward_call(
            where, blocks, places, weights, head, own_rows
        )
        partials = [partial] + [across(partial, k) for k in range(1, group)]
        mine_grad = grad_call(pairs, partials, hidden, head, hidden_units)
        held = (mine_t, mine_grad, swap(other_t), swap(mine_grad))
        if step < ring - 1:
            total = delta_call(total, *held, factor)

    shares = [eval_rows] + [across(eval_rows, k) for k in range(1, group)]
    rows = lax.all_to_all(
        jnp.concatenate(shares, axis=0), ("ring", "core"), split_axis=1, concat_axis=0, tiled=True
    )
    at_spot = jnp.array(spot, jnp.int32)[at_ring]
    order = jnp.array(path, jnp.int32)[(at_spot - 1 - jnp.arange(ring, dtype=jnp.int32)) % ring]
    order = jnp.concatenate([order * 2 + at_core, order * 2 + 1 - at_core]).astype(jnp.int32)

    parts = 2
    momentum_out = None
    rewards = []
    share = rows.shape[0] // replicas
    for part in range(parts):
        momentum_out, near, far = settle_call(
            part, parts, momentum_out, order, where, total, *held,
            momentum, weights, rows, factor, replicas,
        )
        far = swap(far)
        running = near[:share] + far[:share]
        for step in range(1, ring):
            piece = slice(step * share, (step + 1) * share)
            running = along(running) + (near[piece] + far[piece])
        value = running * depth ** (-0.5)
        width = columns // parts
        rewards.append(
            jnp.sum(value * jax.nn.sigmoid(value) * head[:, part * width : (part + 1) * width], axis=1)
        )
    partial = sum(rewards)
    each = partial.shape[0] // group
    result = partial[:each]
    for k in range(1, group):
        result = result + across(partial[k * each : (k + 1) * each], k)
    return (momentum_out, result * hidden_units ** (-0.5))


def solution(mesh):
    replicas, group = mesh.shape["replica"], mesh.shape["fsdp"]
    chips = Mesh(mesh.devices.reshape(replicas // 2, 2, group), ("ring", "core", "fsdp"))
    return jax.shard_map(
        shards,
        mesh=chips,
        in_specs=(
            P(None, "fsdp"),
            P("fsdp"),
            P(("ring", "core"), "fsdp"),
            P(None, ("ring", "core", "fsdp"), None),
            P(None, ("ring", "core"), None),
            P(("ring", "core", "fsdp"), None),
        ),
        out_specs=(P(("ring", "core"), "fsdp"), P(("ring", "core", "fsdp"))),
        check_vma=False,
    )
```

```python
import functools

import jax
import jax.numpy as jnp
from jax import lax
from jax.experimental import pallas as pl
from jax.experimental.pallas import tpu as pltpu
from jax.sharding import Mesh
from jax.sharding import PartitionSpec as P


BLOCK = 128

inner_rate = 300.0
outer_rate = 0.7
outer_decay = 0.9
code_top = 448.0
epsilon = 1e-06

f32 = jnp.float32
bf16 = jnp.bfloat16


def tile_of(extent, top):
    tile = top
    while extent % tile:
        tile //= 2
    return tile


def whole(shape):
    return pl.BlockSpec(shape, lambda *_: (0,) * len(shape))


def params(mib=40):
    return pltpu.CompilerParams(
        dimension_semantics=("arbitrary",), vmem_limit_bytes=mib << 20
    )


def forward_kernel(places, scale, unit_scale, own_rows, first, last, where, *refs):
    blocks = refs[: len(places)]
    w, head = refs[len(places) : len(places) + 2]
    refs = refs[len(places) + 2 :]
    if not first:
        prior = refs[0]
        refs = refs[2:]
    slope, partial = refs[:2]
    refs = refs[2:]
    if first:
        mine_t, other_t = refs[:2]
        refs = refs[2:]
    rows, sums = refs

    @pl.when(pl.program_id(0) == 0)
    def _():
        for (start, size), block in zip(places, blocks):
            rows[start : start + size, :] = block[...]
        sums[...] = jnp.zeros_like(sums) if first else prior[...]
        if first:
            for place, out in ((0, mine_t), (1, other_t)):
                begin = pl.multiple_of(where[place] * own_rows, 128)
                out[...] = rows[:, pl.ds(begin, own_rows)].T

    width = min(256, w.shape[1])
    for start in range(0, w.shape[1], width):
        value = jnp.dot(rows[...], w[:, start : start + width], preferred_element_type=f32) * scale
        weight = head[:, start : start + width]
        squash = jax.nn.sigmoid(value)
        slope[:, start : start + width] = (
            weight * unit_scale * squash * (1.0 + value * (1.0 - squash))
        )
        term = value * squash * weight
        total = sums[...]
        for lane in range(0, width, 128):
            total = total + term[:, lane : lane + 128]
        sums[...] = total

    @pl.when(pl.program_id(0) == pl.num_programs(0) - 1)
    def _():
        if last:
            column = jnp.sum(sums[...], axis=1, keepdims=True)
            partial[...] = jnp.broadcast_to(column, sums.shape).T[0:1, :]
        else:
            partial[...] = sums[...]


def places_of(blocks):
    places = []
    for item in blocks:
        places.append((sum(size for _, size in places), item.shape[0]))
    return places


def cut_kernel(places, where, *refs):
    for (start, size), block in zip(places, refs):
        refs[-1][start : start + size, :] = block[...]


def cut_call(where, blocks, width):
    places = places_of(blocks)
    count = sum(size for _, size in places)
    return pl.pallas_call(
        functools.partial(cut_kernel, places),
        out_shape=jax.ShapeDtypeStruct((count, width), bf16),
        grid_spec=pltpu.PrefetchScalarGridSpec(
            num_scalar_prefetch=1,
            grid=(1,),
            in_specs=[
                pl.BlockSpec((size, width), lambda j, where: (0, where[2])) for _, size in places
            ],
            out_specs=whole((count, width)),
        ),
        compiler_params=params(8),
        cost_estimate=pl.CostEstimate(flops=0, bytes_accessed=4 * count * width, transcendentals=0),
    )(where, *blocks)


def join_kernel(places, *refs):
    for (start, size), item in zip(places, refs):
        refs[-1][:, start : start + size] = item[...]


def join_call(items):
    places, start = [], 0
    for item in items:
        places.append((start, item.shape[1]))
        start += item.shape[1]
    shape = (items[0].shape[0], start)
    return pl.pallas_call(
        functools.partial(join_kernel, places),
        out_shape=jax.ShapeDtypeStruct(shape, bf16),
        grid=(1,),
        in_specs=[whole(item.shape) for item in items],
        out_specs=whole(shape),
        compiler_params=params(16),
        cost_estimate=pl.CostEstimate(
            flops=0, bytes_accessed=4 * shape[0] * shape[1], transcendentals=0
        ),
    )(*items)


def turn_kernel(where, mine, other, mine_t, other_t):
    mine_t[...] = mine[...].T
    other_t[...] = other[...].T


def turn_call(where, piece):
    count, width = piece.shape[0], piece.shape[1] // 2
    return pl.pallas_call(
        turn_kernel,
        out_shape=[jax.ShapeDtypeStruct((width, count), bf16)] * 2,
        grid_spec=pltpu.PrefetchScalarGridSpec(
            num_scalar_prefetch=1,
            grid=(1,),
            in_specs=[
                pl.BlockSpec((count, width), lambda j, where: (0, where[3])),
                pl.BlockSpec((count, width), lambda j, where: (0, where[4])),
            ],
            out_specs=[whole((width, count))] * 2,
        ),
        compiler_params=params(8),
        cost_estimate=pl.CostEstimate(flops=0, bytes_accessed=8 * count * width, transcendentals=0),
    )(where, piece, piece)


def forward_call(
    where, blocks, places, weights, head, hidden_units, own_rows, tile, begin, end, prior, slope
):
    depth, columns = weights.shape
    last = end * tile == columns
    count = sum(size for _, size in places)
    width = (end - begin) * tile
    first = prior is None
    turned = (own_rows, count)
    sums = (1, count) if last else (count, 128)
    n_blocks = len(blocks)
    return pl.pallas_call(
        functools.partial(
            forward_kernel, places, depth ** (-0.5), hidden_units ** (-0.5), own_rows, first, last
        ),
        out_shape=[
            jax.ShapeDtypeStruct((count, columns), f32),
            jax.ShapeDtypeStruct(sums, f32),
        ]
        + [jax.ShapeDtypeStruct(turned, bf16)] * (2 if first else 0),
        grid_spec=pltpu.PrefetchScalarGridSpec(
            num_scalar_prefetch=1,
            grid=(end - begin,),
            in_specs=[whole(block.shape) for block in blocks]
            + [
                pl.BlockSpec((depth, tile), lambda j, *_: (0, begin + j)),
                pl.BlockSpec((1, tile), lambda j, *_: (0, begin + j)),
            ]
            + ([] if first else [whole((count, 128)), pl.BlockSpec(memory_space=pl.ANY)]),
            out_specs=[
                pl.BlockSpec((count, tile), lambda j, *_: (0, begin + j)),
                whole(sums),
            ]
            + [whole(turned)] * (2 if first else 0),
            scratch_shapes=[
                pltpu.VMEM((count, depth), bf16),
                pltpu.VMEM((count, 128), f32),
            ],
        ),
        input_output_aliases={} if first else {n_blocks + 4: 0},
        compiler_params=params(30),
        cost_estimate=pl.CostEstimate(
            flops=2 * count * depth * width,
            bytes_accessed=2 * depth * width + 4 * count * width,
            transcendentals=count * width,
        ),
    )(where, *blocks, weights, head, *(() if first else (prior, slope)))


def grad_kernel(group, scale, replicas, *refs):
    pairs = refs[:replicas]
    partials = refs[replicas : replicas + group]
    slope, out, reward_grad = refs[replicas + group :]

    @pl.when(pl.program_id(0) == 0)
    def _():
        n_pairs = pairs[0].shape[1]
        rows = reward_grad.shape[0] // len(pairs)
        size = rows // group
        columns = [
            jnp.broadcast_to(partial[...], (n_pairs, reward_grad.shape[0])).T for partial in partials
        ]
        for at, pair in enumerate(pairs):
            rewards = jnp.zeros((rows, n_pairs), f32)
            for k, column in enumerate(columns):
                starts = [at * rows + (j ^ k) * size for j in range(group)]
                rewards = rewards + jnp.concatenate([column[b : b + size] for b in starts], axis=0)
            rewards = rewards * scale
            position = lax.broadcasted_iota(jnp.int32, (rows, n_pairs), 0)
            table = (position == pair[1:2, :]).astype(f32) - (position == pair[0:1, :]).astype(f32)
            gap = jnp.sum(table * rewards, axis=0, keepdims=True)
            pair_weight = jax.nn.sigmoid(gap)
            column = jnp.sum(table * pair_weight, axis=1, keepdims=True)
            reward_grad[at * rows : (at + 1) * rows, :] = jnp.broadcast_to(column, (rows, 128))

    out[...] = (reward_grad[:, 0:1] * slope[...]).astype(bf16)


def grad_call(pairs, partials, slope, hidden_units, tile, begin, end):
    rows = slope.shape[0]
    mib = 20
    columns = (end - begin) * tile
    offset = 0
    if begin == 0 and end % 2 == 1 and (end * tile) % 256 == 0 and columns == slope.shape[1]:
        tile = columns // 2
    elif begin % (end - begin) == 0:
        offset, tile = begin // (end - begin), columns
    else:
        offset = begin
    return pl.pallas_call(
        functools.partial(grad_kernel, len(partials), hidden_units ** (-0.5), len(pairs)),
        out_shape=jax.ShapeDtypeStruct((rows, columns), bf16),
        grid=(columns // tile,),
        in_specs=[whole(pair.shape) for pair in pairs]
        + [whole(partial.shape) for partial in partials]
        + [pl.BlockSpec((rows, tile), lambda j: (0, offset + j))],
        out_specs=pl.BlockSpec((rows, tile), lambda j: (0, j)),
        scratch_shapes=[pltpu.VMEM((rows, 128), f32)],
        compiler_params=params(mib),
        cost_estimate=pl.CostEstimate(
            flops=2 * rows * columns, bytes_accessed=6 * rows * columns, transcendentals=0
        ),
    )(*pairs, *partials, slope)


def coded_sum(x_t, grads, span, start, factor):
    raws, column = [], 0
    for grad in grads:
        for at in range(0, grad.shape[0], span):
            rows = x_t[start : start + BLOCK, column : column + span]
            raws.append(jnp.dot(rows, grad[at : at + span, :], preferred_element_type=f32))
            column += span
    largest = jnp.concatenate(
        [jnp.max(jnp.abs(raw), axis=0, keepdims=True) for raw in raws], axis=0
    )
    scale = ((largest * factor + epsilon) / code_top).astype(bf16).astype(f32)
    inverse = factor / scale
    total = None
    for k, raw in enumerate(raws):
        coded = (raw * inverse[k : k + 1]).astype(bf16)
        decoded = coded.astype(f32) * scale[k : k + 1]
        total = decoded if total is None else total + decoded
    return total


def settle_kernel(chained, n_grads, span, factor, replicas, order, where, *refs):
    if chained:
        refs = refs[1:]
    x_t, grads = refs[0], refs[1 : 1 + n_grads]
    momentum, w, rows, momentum_out, near, far, sorted_rows, new_w = refs[1 + n_grads :]
    slots = order.shape[0]
    size = rows.shape[0] // slots

    @pl.when(pl.program_id(0) == 0)
    def _():
        for slot in range(slots):
            begin = pl.multiple_of(order[slot] * size, size)
            sorted_rows[slot * size : (slot + 1) * size, :] = rows[pl.ds(begin, size), :]

    updates = []
    for start in range(0, momentum.shape[0], BLOCK):
        part = slice(start, start + BLOCK)
        pseudo = coded_sum(x_t, grads, span, start, factor) * (1.0 / replicas)
        moved = outer_decay * momentum[part, :] + pseudo
        momentum_out[part, :] = moved
        updates.append(outer_rate * (pseudo + outer_decay * moved))
    largest = jnp.concatenate(
        [jnp.max(jnp.abs(update), axis=0, keepdims=True) for update in updates], axis=0
    )
    scale = ((largest + epsilon) / code_top).astype(bf16).astype(f32)
    inverse = 1.0 / scale
    for k, update in enumerate(updates):
        part = slice(k * BLOCK, (k + 1) * BLOCK)
        coded = (update * inverse[k : k + 1]).astype(bf16)
        decoded = coded.astype(f32) * scale[k : k + 1]
        new_w[part, :] = (w[part, :].astype(f32) - decoded).astype(bf16)
    value = jnp.dot(sorted_rows[...], new_w[...], preferred_element_type=f32)
    half = value.shape[0] // 2
    near[...] = value[:half]
    far[...] = value[half:]


def settle_call(
    chain, order, where, x_t, terms, momentum, weights, rows, span, factor, replicas, tile, begin, end
):
    own_rows, columns = momentum.shape
    width = (end - begin) * tile
    chained = chain is not None
    local = lambda j, *_: (0, j)
    down = lambda j, *_: (0, begin + j)
    out_rows = rows.shape[0] // 2
    term_specs = [whole(x_t.shape)]
    for grad, start in terms:
        place = lambda j, *_, start=start: (0, start + j)
        term_specs.append(pl.BlockSpec((grad.shape[0], tile), place))
    depth = x_t.shape[1]
    return pl.pallas_call(
        functools.partial(settle_kernel, chained, len(terms), span, factor, replicas),
        out_shape=(
            jax.ShapeDtypeStruct((own_rows, columns), f32),
            jax.ShapeDtypeStruct((out_rows, width), f32),
            jax.ShapeDtypeStruct((out_rows, width), f32),
        ),
        grid_spec=pltpu.PrefetchScalarGridSpec(
            num_scalar_prefetch=2,
            grid=(end - begin,),
            in_specs=([pl.BlockSpec(memory_space=pl.ANY)] if chained else [])
            + term_specs
            + [
                pl.BlockSpec((own_rows, tile), down),
                pl.BlockSpec((own_rows, tile), lambda j, order, where: (where[0], begin + j)),
                whole(rows.shape),
            ],
            out_specs=[
                pl.BlockSpec((own_rows, tile), down),
                pl.BlockSpec((out_rows, tile), local),
                pl.BlockSpec((out_rows, tile), local),
            ],
            scratch_shapes=[
                pltpu.VMEM(rows.shape, bf16),
                pltpu.VMEM((own_rows, tile), bf16),
            ],
        ),
        input_output_aliases={2: 0} if chained else {},
        compiler_params=params(40),
        cost_estimate=pl.CostEstimate(
            flops=(2 * own_rows * depth + 2 * own_rows * rows.shape[0]) * width,
            bytes_accessed=(10 * own_rows + 2 * depth + 4 * rows.shape[0]) * width,
            transcendentals=0,
        ),
    )(
        order, where, *((chain,) if chained else ()), x_t, *(grad for grad, _ in terms),
        momentum, weights, rows,
    )


def shards(weights, head_vector, momentum, batches, pair_index, eval_rows):
    ring, group = lax.axis_size("ring"), lax.axis_size("fsdp")
    replicas = 2 * ring
    depth, columns = weights.shape
    hidden_units = columns * group
    own_rows = momentum.shape[0]
    block = batches.shape[1]
    span = block * group
    at_ring, at_core, at_fsdp = (lax.axis_index(name) for name in ("ring", "core", "fsdp"))
    path = list(range(0, 1)) + list(range(1, ring, 2)) + list(range(2, ring, 2))[::-1]
    onward = [(path[i], path[(i + 1) % ring]) for i in range(ring)]
    at_spot = jnp.where(at_ring % 2 == 1, (at_ring + 1) // 2, (ring - at_ring // 2) % ring)

    def chip_at(spot):
        return jnp.where(spot == 0, 0, jnp.where(spot <= ring // 2, 2 * spot - 1, 2 * (ring - spot)))

    tile = tile_of(columns, 512)
    tiles = columns // tile
    first, second = (3 * tiles + 6) // 7, (5 * tiles + 6) // 7
    outer_cuts = [cut for cut in ((0, first), (first, second), (second, tiles)) if cut[0] < cut[1]]

    def along(value):
        return lax.ppermute(value, "ring", onward)

    def across(value, k):
        return lax.ppermute(value, "fsdp", [(i, i ^ k) for i in range(group)])

    def back(value):
        return lax.ppermute(value, "ring", [(b, a) for a, b in onward])

    def swap(value):
        return lax.ppermute(value, "core", [(0, 1), (1, 0)])

    replica = at_ring * 2 + at_core
    before = chip_at((at_spot - 1) % ring)
    where = jnp.stack([replica, at_ring * 2 + 1 - at_core, before, at_core, 1 - at_core]).astype(jnp.int32)
    head = head_vector.reshape(1, columns)

    pairs = pair_index[0].T
    pairs = [((pairs // block) ^ at_fsdp) * block + pairs % block]
    for hop in range(1, ring - 1):
        pairs.append(
            lax.ppermute(pairs[0], "ring", [(path[i], path[(i + hop) % ring]) for i in range(ring)])
        )

    half = block // 2
    steps = []
    own = batches[0]
    for step in range(ring - 1):
        if step:
            own = along(own)
        if group != 4:
            steps.append([own] + [across(own, k) for k in range(1, group)])
        elif step == 0:
            up, low = own[:half], own[half:]
            one = [across(up, 1), across(low, 1)]
            two = [across(up, 2), across(low, 2)]
            last = [across(one[0], 2), across(two[1], 1)]
            steps.append([own] + one + two + last)
        else:
            sides = [across(own, 1), across(own, 2)]
            if step == 1:
                last = [along(steps[0][-2]), along(steps[0][-1])]
            else:
                last = [across(own, 3)]
            steps.append([own] + sides + last)

    shares = [eval_rows] + [across(eval_rows, k) for k in range(1, group)]
    rows = lax.all_to_all(
        jnp.concatenate(shares, axis=0), ("ring", "core"), split_axis=1, concat_axis=0, tiled=True
    )
    order = chip_at((at_spot - 1 - jnp.arange(ring, dtype=jnp.int32)) % ring)
    order = jnp.concatenate([order * 2 + at_core, order * 2 + 1 - at_core]).astype(jnp.int32)
    where, order = lax.optimization_barrier((where, order))


    factor = inner_rate * depth ** (-0.5)
    terms = []
    piece = cut_call(where, steps[0], 2 * own_rows)
    piece = back(piece)
    next_t, next_other_t = turn_call(where, piece)
    chunks = [[0]] + [[step, step + 1] for step in range(1, ring - 1, 2)]
    for chunk in chunks:
        name = chunk[0]
        blocks = [item for step in chunk for item in steps[step]]
        places = places_of(blocks)
        slope = partial = None
        for begin, end in [(0, tiles)]:
            outs = forward_call(
                where, blocks, places, weights, head, hidden_units, own_rows, tile, begin, end,
                partial, slope,
            )
            slope, partial = outs[:2]
            if begin == 0:
                mine_t, other_t = outs[2:]
        partials = [partial] + [across(partial, k) for k in range(1, group)]
        other_t = swap(other_t)
        chunk_pairs = [pairs[step] for step in chunk]
        last = chunk is chunks[-1]
        mine_parts, other_parts = [], []
        for begin, end in outer_cuts if last else [(0, tiles)]:
            part = grad_call(chunk_pairs, partials, slope, hidden_units, tile, begin, end)
            mine_parts.append(part)
            other_parts.append(swap(part))
        terms += [(mine_t, mine_parts), (other_t, other_parts)]
        if name == 0:
            next_grad = back(mine_parts[0])
    terms += [(next_t, [next_grad]), (swap(next_other_t), [swap(next_grad)])]

    x_t = join_call([item for item, _ in terms])
    momentum_out = None
    rewards = []
    share = rows.shape[0] // replicas
    for index, (begin, end) in enumerate(outer_cuts):
        part_terms = [
            (parts[index], 0) if len(parts) > 1 else (parts[0], begin) for _, parts in terms
        ]
        momentum_out, near, far = settle_call(
            momentum_out, order, where, x_t, part_terms, momentum, weights, rows, span, factor, replicas,
            tile, begin, end,
        )
        far = swap(far)
        running = near[-share:] + far[-share:]
        for hop in range(1, ring):
            piece = slice((ring - 1 - hop) * share, (ring - hop) * share)
            got = lax.ppermute(
                (near[piece] + far[piece]).astype(bf16),
                "ring",
                [(path[i], path[(i + hop) % ring]) for i in range(ring)],
            )
            running = running + got.astype(f32)
        value = running * depth ** (-0.5)
        rewards.append(
            jnp.sum(value * jax.nn.sigmoid(value) * head[:, begin * tile : end * tile], axis=1)
        )
    partial = sum(rewards)
    each = partial.shape[0] // group
    result = partial[:each]
    for k in range(1, group):
        result = result + across(partial[k * each : (k + 1) * each], k)
    return (momentum_out, result * hidden_units ** (-0.5))


def solution(mesh):
    replicas, group = mesh.shape["replica"], mesh.shape["fsdp"]
    chips = Mesh(mesh.devices.reshape(replicas // 2, 2, group), ("ring", "core", "fsdp"))

    return jax.shard_map(
        shards,
        mesh=chips,
        in_specs=(
            P(None, "fsdp"),
            P("fsdp"),
            P(("ring", "core"), "fsdp"),
            P(None, ("ring", "core", "fsdp"), None),
            P(None, ("ring", "core"), None),
            P(("ring", "core", "fsdp"), None),
        ),
        out_specs=(P(("ring", "core"), "fsdp"), P(("ring", "core", "fsdp"))),
        check_vma=False,
    )
```

```python
import functools

import jax
import jax.numpy as jnp
from jax import lax
from jax.experimental import pallas as pl
from jax.experimental.pallas import tpu as pltpu
from jax.sharding import Mesh
from jax.sharding import PartitionSpec as P


BLOCK = 128

inner_rate = 300.0
outer_rate = 0.7
outer_decay = 0.9
code_top = 448.0
epsilon = 1e-06

f32 = jnp.float32
bf16 = jnp.bfloat16


def tile_of(extent, top):
    tile = top
    while extent % tile:
        tile //= 2
    return tile


def whole(shape):
    return pl.BlockSpec(shape, lambda *_: (0,) * len(shape))


def params(mib=40):
    return pltpu.CompilerParams(
        dimension_semantics=("arbitrary",), vmem_limit_bytes=mib << 20
    )


def forward_kernel(places, scale, unit_scale, own_rows, first, last, where, *refs):
    blocks = refs[: len(places)]
    w, head = refs[len(places) : len(places) + 2]
    refs = refs[len(places) + 2 :]
    if not first:
        prior = refs[0]
        refs = refs[2:]
    slope, partial = refs[:2]
    refs = refs[2:]
    if first:
        mine_t, other_t = refs[:2]
        refs = refs[2:]
    rows, sums = refs

    @pl.when(pl.program_id(0) == 0)
    def _():
        for (start, size), block in zip(places, blocks):
            rows[start : start + size, :] = block[...]
        sums[...] = jnp.zeros_like(sums) if first else prior[...]
        if first:
            for place, out in ((0, mine_t), (1, other_t)):
                begin = pl.multiple_of(where[place] * own_rows, 128)
                out[...] = rows[:, pl.ds(begin, own_rows)].T

    width = min(256, w.shape[1])
    for start in range(0, w.shape[1], width):
        value = jnp.dot(rows[...], w[:, start : start + width], preferred_element_type=f32) * scale
        weight = head[:, start : start + width]
        squash = jax.nn.sigmoid(value)
        slope[:, start : start + width] = (
            weight * unit_scale * squash * (1.0 + value * (1.0 - squash))
        )
        term = value * squash * weight
        total = sums[...]
        for lane in range(0, width, 128):
            total = total + term[:, lane : lane + 128]
        sums[...] = total

    @pl.when(pl.program_id(0) == pl.num_programs(0) - 1)
    def _():
        if last:
            column = jnp.sum(sums[...], axis=1, keepdims=True)
            partial[...] = jnp.broadcast_to(column, sums.shape).T[0:1, :]
        else:
            partial[...] = sums[...]


def places_of(blocks):
    places = []
    for item in blocks:
        places.append((sum(size for _, size in places), item.shape[0]))
    return places


def cut_kernel(places, where, *refs):
    for (start, size), block in zip(places, refs):
        refs[-1][start : start + size, :] = block[...]


def cut_call(where, blocks, width):
    places = places_of(blocks)
    count = sum(size for _, size in places)
    return pl.pallas_call(
        functools.partial(cut_kernel, places),
        out_shape=jax.ShapeDtypeStruct((count, width), bf16),
        grid_spec=pltpu.PrefetchScalarGridSpec(
            num_scalar_prefetch=1,
            grid=(1,),
            in_specs=[
                pl.BlockSpec((size, width), lambda j, where: (0, where[2])) for _, size in places
            ],
            out_specs=whole((count, width)),
        ),
        compiler_params=params(8),
        cost_estimate=pl.CostEstimate(flops=0, bytes_accessed=4 * count * width, transcendentals=0),
    )(where, *blocks)


def join_kernel(places, *refs):
    for (start, size), item in zip(places, refs):
        refs[-1][:, start : start + size] = item[...]


def join_call(items):
    places, start = [], 0
    for item in items:
        places.append((start, item.shape[1]))
        start += item.shape[1]
    shape = (items[0].shape[0], start)
    return pl.pallas_call(
        functools.partial(join_kernel, places),
        out_shape=jax.ShapeDtypeStruct(shape, bf16),
        grid=(1,),
        in_specs=[whole(item.shape) for item in items],
        out_specs=whole(shape),
        compiler_params=params(16),
        cost_estimate=pl.CostEstimate(
            flops=0, bytes_accessed=4 * shape[0] * shape[1], transcendentals=0
        ),
    )(*items)


def turn_kernel(where, mine, other, mine_t, other_t):
    mine_t[...] = mine[...].T
    other_t[...] = other[...].T


def turn_call(where, piece):
    count, width = piece.shape[0], piece.shape[1] // 2
    return pl.pallas_call(
        turn_kernel,
        out_shape=[jax.ShapeDtypeStruct((width, count), bf16)] * 2,
        grid_spec=pltpu.PrefetchScalarGridSpec(
            num_scalar_prefetch=1,
            grid=(1,),
            in_specs=[
                pl.BlockSpec((count, width), lambda j, where: (0, where[3])),
                pl.BlockSpec((count, width), lambda j, where: (0, where[4])),
            ],
            out_specs=[whole((width, count))] * 2,
        ),
        compiler_params=params(8),
        cost_estimate=pl.CostEstimate(flops=0, bytes_accessed=8 * count * width, transcendentals=0),
    )(where, piece, piece)


def forward_call(
    where, blocks, places, weights, head, hidden_units, own_rows, tile, begin, end, prior, slope
):
    depth, columns = weights.shape
    last = end * tile == columns
    count = sum(size for _, size in places)
    width = (end - begin) * tile
    first = prior is None
    turned = (own_rows, count)
    sums = (1, count) if last else (count, 128)
    n_blocks = len(blocks)
    return pl.pallas_call(
        functools.partial(
            forward_kernel, places, depth ** (-0.5), hidden_units ** (-0.5), own_rows, first, last
        ),
        out_shape=[
            jax.ShapeDtypeStruct((count, columns), f32),
            jax.ShapeDtypeStruct(sums, f32),
        ]
        + [jax.ShapeDtypeStruct(turned, bf16)] * (2 if first else 0),
        grid_spec=pltpu.PrefetchScalarGridSpec(
            num_scalar_prefetch=1,
            grid=(end - begin,),
            in_specs=[whole(block.shape) for block in blocks]
            + [
                pl.BlockSpec((depth, tile), lambda j, *_: (0, begin + j)),
                pl.BlockSpec((1, tile), lambda j, *_: (0, begin + j)),
            ]
            + ([] if first else [whole((count, 128)), pl.BlockSpec(memory_space=pl.ANY)]),
            out_specs=[
                pl.BlockSpec((count, tile), lambda j, *_: (0, begin + j)),
                whole(sums),
            ]
            + [whole(turned)] * (2 if first else 0),
            scratch_shapes=[
                pltpu.VMEM((count, depth), bf16),
                pltpu.VMEM((count, 128), f32),
            ],
        ),
        input_output_aliases={} if first else {n_blocks + 4: 0},
        compiler_params=params(30),
        cost_estimate=pl.CostEstimate(
            flops=2 * count * depth * width,
            bytes_accessed=2 * depth * width + 4 * count * width,
            transcendentals=count * width,
        ),
    )(where, *blocks, weights, head, *(() if first else (prior, slope)))


def grad_kernel(group, scale, replicas, *refs):
    pairs = refs[:replicas]
    partials = refs[replicas : replicas + group]
    slope, out, reward_grad = refs[replicas + group :]

    @pl.when(pl.program_id(0) == 0)
    def _():
        n_pairs = pairs[0].shape[1]
        rows = reward_grad.shape[0] // len(pairs)
        size = rows // group
        columns = [
            jnp.broadcast_to(partial[...], (n_pairs, reward_grad.shape[0])).T for partial in partials
        ]
        for at, pair in enumerate(pairs):
            rewards = jnp.zeros((rows, n_pairs), f32)
            for k, column in enumerate(columns):
                starts = [at * rows + (j ^ k) * size for j in range(group)]
                rewards = rewards + jnp.concatenate([column[b : b + size] for b in starts], axis=0)
            rewards = rewards * scale
            position = lax.broadcasted_iota(jnp.int32, (rows, n_pairs), 0)
            table = (position == pair[1:2, :]).astype(f32) - (position == pair[0:1, :]).astype(f32)
            gap = jnp.sum(table * rewards, axis=0, keepdims=True)
            pair_weight = jax.nn.sigmoid(gap)
            column = jnp.sum(table * pair_weight, axis=1, keepdims=True)
            reward_grad[at * rows : (at + 1) * rows, :] = jnp.broadcast_to(column, (rows, 128))

    out[...] = (reward_grad[:, 0:1] * slope[...]).astype(bf16)


def grad_call(pairs, partials, slope, hidden_units, tile, begin, end):
    rows = slope.shape[0]
    mib = 20
    columns = (end - begin) * tile
    offset = 0
    if begin == 0 and end % 2 == 1 and (end * tile) % 256 == 0 and columns == slope.shape[1]:
        tile = columns // 2
    elif begin % (end - begin) == 0:
        offset, tile = begin // (end - begin), columns
    else:
        offset = begin
    return pl.pallas_call(
        functools.partial(grad_kernel, len(partials), hidden_units ** (-0.5), len(pairs)),
        out_shape=jax.ShapeDtypeStruct((rows, columns), bf16),
        grid=(columns // tile,),
        in_specs=[whole(pair.shape) for pair in pairs]
        + [whole(partial.shape) for partial in partials]
        + [pl.BlockSpec((rows, tile), lambda j: (0, offset + j))],
        out_specs=pl.BlockSpec((rows, tile), lambda j: (0, j)),
        scratch_shapes=[pltpu.VMEM((rows, 128), f32)],
        compiler_params=params(mib),
        cost_estimate=pl.CostEstimate(
            flops=2 * rows * columns, bytes_accessed=6 * rows * columns, transcendentals=0
        ),
    )(*pairs, *partials, slope)


def coded_sum(x_t, grads, span, start, factor):
    raws, column = [], 0
    for grad in grads:
        for at in range(0, grad.shape[0], span):
            rows = x_t[start : start + BLOCK, column : column + span]
            raws.append(jnp.dot(rows, grad[at : at + span, :], preferred_element_type=f32))
            column += span
    largest = jnp.concatenate(
        [jnp.max(jnp.abs(raw), axis=0, keepdims=True) for raw in raws], axis=0
    )
    scale = ((largest * factor + epsilon) / code_top).astype(bf16).astype(f32)
    inverse = factor / scale
    total = None
    for k, raw in enumerate(raws):
        coded = (raw * inverse[k : k + 1]).astype(bf16)
        decoded = coded.astype(f32) * scale[k : k + 1]
        total = decoded if total is None else total + decoded
    return total


def settle_kernel(chained, n_grads, span, factor, replicas, order, where, *refs):
    if chained:
        refs = refs[1:]
    x_t, grads = refs[0], refs[1 : 1 + n_grads]
    momentum, w, rows, momentum_out, near, far, sorted_rows, new_w = refs[1 + n_grads :]
    slots = order.shape[0]
    size = rows.shape[0] // slots

    @pl.when(pl.program_id(0) == 0)
    def _():
        for slot in range(slots):
            begin = pl.multiple_of(order[slot] * size, size)
            sorted_rows[slot * size : (slot + 1) * size, :] = rows[pl.ds(begin, size), :]

    updates = []
    for start in range(0, momentum.shape[0], BLOCK):
        part = slice(start, start + BLOCK)
        pseudo = coded_sum(x_t, grads, span, start, factor) * (1.0 / replicas)
        moved = outer_decay * momentum[part, :] + pseudo
        momentum_out[part, :] = moved
        updates.append(outer_rate * (pseudo + outer_decay * moved))
    largest = jnp.concatenate(
        [jnp.max(jnp.abs(update), axis=0, keepdims=True) for update in updates], axis=0
    )
    scale = ((largest + epsilon) / code_top).astype(bf16).astype(f32)
    inverse = 1.0 / scale
    for k, update in enumerate(updates):
        part = slice(k * BLOCK, (k + 1) * BLOCK)
        coded = (update * inverse[k : k + 1]).astype(bf16)
        decoded = coded.astype(f32) * scale[k : k + 1]
        new_w[part, :] = (w[part, :].astype(f32) - decoded).astype(bf16)
    value = jnp.dot(sorted_rows[...], new_w[...], preferred_element_type=f32)
    half = value.shape[0] // 2
    near[...] = value[:half]
    far[...] = value[half:]


def settle_call(
    chain, order, where, x_t, terms, momentum, weights, rows, span, factor, replicas, tile, begin, end
):
    own_rows, columns = momentum.shape
    width = (end - begin) * tile
    chained = chain is not None
    local = lambda j, *_: (0, j)
    down = lambda j, *_: (0, begin + j)
    out_rows = rows.shape[0] // 2
    term_specs = [whole(x_t.shape)]
    for grad, start in terms:
        place = lambda j, *_, start=start: (0, start + j)
        term_specs.append(pl.BlockSpec((grad.shape[0], tile), place))
    depth = x_t.shape[1]
    return pl.pallas_call(
        functools.partial(settle_kernel, chained, len(terms), span, factor, replicas),
        out_shape=(
            jax.ShapeDtypeStruct((own_rows, columns), f32),
            jax.ShapeDtypeStruct((out_rows, width), f32),
            jax.ShapeDtypeStruct((out_rows, width), f32),
        ),
        grid_spec=pltpu.PrefetchScalarGridSpec(
            num_scalar_prefetch=2,
            grid=(end - begin,),
            in_specs=([pl.BlockSpec(memory_space=pl.ANY)] if chained else [])
            + term_specs
            + [
                pl.BlockSpec((own_rows, tile), down),
                pl.BlockSpec((own_rows, tile), lambda j, order, where: (where[0], begin + j)),
                whole(rows.shape),
            ],
            out_specs=[
                pl.BlockSpec((own_rows, tile), down),
                pl.BlockSpec((out_rows, tile), local),
                pl.BlockSpec((out_rows, tile), local),
            ],
            scratch_shapes=[
                pltpu.VMEM(rows.shape, bf16),
                pltpu.VMEM((own_rows, tile), bf16),
            ],
        ),
        input_output_aliases={2: 0} if chained else {},
        compiler_params=params(40),
        cost_estimate=pl.CostEstimate(
            flops=(2 * own_rows * depth + 2 * own_rows * rows.shape[0]) * width,
            bytes_accessed=(10 * own_rows + 2 * depth + 4 * rows.shape[0]) * width,
            transcendentals=0,
        ),
    )(
        order, where, *((chain,) if chained else ()), x_t, *(grad for grad, _ in terms),
        momentum, weights, rows,
    )


def shards(weights, head_vector, momentum, batches, pair_index, eval_rows):
    ring, group = lax.axis_size("ring"), lax.axis_size("fsdp")
    replicas = 2 * ring
    depth, columns = weights.shape
    hidden_units = columns * group
    own_rows = momentum.shape[0]
    block = batches.shape[1]
    span = block * group
    at_ring, at_core, at_fsdp = (lax.axis_index(name) for name in ("ring", "core", "fsdp"))
    path = list(range(0, 1)) + list(range(1, ring, 2)) + list(range(2, ring, 2))[::-1]
    onward = [(path[i], path[(i + 1) % ring]) for i in range(ring)]
    at_spot = jnp.where(at_ring % 2 == 1, (at_ring + 1) // 2, (ring - at_ring // 2) % ring)

    def chip_at(spot):
        return jnp.where(spot == 0, 0, jnp.where(spot <= ring // 2, 2 * spot - 1, 2 * (ring - spot)))

    tile = tile_of(columns, 512)
    tiles = columns // tile
    first, second = (3 * tiles + 6) // 7, (5 * tiles + 6) // 7
    outer_cuts = [cut for cut in ((0, first), (first, second), (second, tiles)) if cut[0] < cut[1]]

    def along(value):
        return lax.ppermute(value, "ring", onward)

    def across(value, k):
        return lax.ppermute(value, "fsdp", [(i, i ^ k) for i in range(group)])

    def back(value):
        return lax.ppermute(value, "ring", [(b, a) for a, b in onward])

    def swap(value):
        return lax.ppermute(value, "core", [(0, 1), (1, 0)])

    replica = at_ring * 2 + at_core
    before = chip_at((at_spot - 1) % ring)
    where = jnp.stack([replica, at_ring * 2 + 1 - at_core, before, at_core, 1 - at_core]).astype(jnp.int32)
    head = head_vector.reshape(1, columns)

    pairs = pair_index[0].T
    pairs = [((pairs // block) ^ at_fsdp) * block + pairs % block]
    for hop in range(1, ring - 1):
        pairs.append(
            lax.ppermute(pairs[0], "ring", [(path[i], path[(i + hop) % ring]) for i in range(ring)])
        )

    half = block // 2
    steps = []
    own = batches[0]
    for step in range(ring - 1):
        if step:
            own = along(own)
        if group != 4:
            steps.append([own] + [across(own, k) for k in range(1, group)])
        elif step == 0:
            up, low = own[:half], own[half:]
            one = [across(up, 1), across(low, 1)]
            two = [across(up, 2), across(low, 2)]
            last = [across(one[0], 2), across(two[1], 1)]
            steps.append([own] + one + two + last)
        else:
            sides = [across(own, 1), across(own, 2)]
            if step == 1:
                last = [along(steps[0][-2]), along(steps[0][-1])]
            else:
                last = [across(own, 3)]
            steps.append([own] + sides + last)

    shares = [eval_rows] + [across(eval_rows, k) for k in range(1, group)]
    rows = lax.all_to_all(
        jnp.concatenate(shares, axis=0), ("ring", "core"), split_axis=1, concat_axis=0, tiled=True
    )
    order = chip_at((at_spot - 1 - jnp.arange(ring, dtype=jnp.int32)) % ring)
    order = jnp.concatenate([order * 2 + at_core, order * 2 + 1 - at_core]).astype(jnp.int32)
    where, order = lax.optimization_barrier((where, order))


    factor = inner_rate * depth ** (-0.5)
    terms = []
    piece = cut_call(where, steps[0], 2 * own_rows)
    piece = back(piece)
    next_t, next_other_t = turn_call(where, piece)
    chunks = [[0]] + [[step, step + 1] for step in range(1, ring - 1, 2)]
    for chunk in chunks:
        name = chunk[0]
        blocks = [item for step in chunk for item in steps[step]]
        places = places_of(blocks)
        slope = partial = None
        for begin, end in [(0, tiles)]:
            outs = forward_call(
                where, blocks, places, weights, head, hidden_units, own_rows, tile, begin, end,
                partial, slope,
            )
            slope, partial = outs[:2]
            if begin == 0:
                mine_t, other_t = outs[2:]
        partials = [partial] + [across(partial, k) for k in range(1, group)]
        other_t = swap(other_t)
        chunk_pairs = [pairs[step] for step in chunk]
        if chunk is chunks[-1]:
            part_cuts = outer_cuts
        elif name == 0:
            part_cuts = [cut for cut in ((0, first), (first, tiles)) if cut[0] < cut[1]]
        else:
            part_cuts = [(0, tiles)]
        mine_parts, other_parts = [], []
        for begin, end in part_cuts:
            part = grad_call(chunk_pairs, partials, slope, hidden_units, tile, begin, end)
            mine_parts.append((part, begin))
            other_parts.append((swap(part), begin))
        terms += [(mine_t, mine_parts), (other_t, other_parts)]
        if name == 0:
            next_parts = [(back(part), begin) for part, begin in mine_parts]
    swapped_parts = [(swap(part), begin) for part, begin in next_parts]
    terms += [(next_t, next_parts), (swap(next_other_t), swapped_parts)]

    x_t = join_call([item for item, _ in terms])
    momentum_out = None
    rewards = []
    share = rows.shape[0] // replicas
    for begin, end in outer_cuts:
        part_terms = []
        for _, parts in terms:
            grad, start = [part for part in parts if part[1] <= begin][-1]
            part_terms.append((grad, begin - start))
        momentum_out, near, far = settle_call(
            momentum_out, order, where, x_t, part_terms, momentum, weights, rows, span, factor, replicas,
            tile, begin, end,
        )
        far = swap(far)
        running = near[-share:] + far[-share:]
        for hop in range(1, ring):
            piece = slice((ring - 1 - hop) * share, (ring - hop) * share)
            got = lax.ppermute(
                (near[piece] + far[piece]).astype(bf16),
                "ring",
                [(path[i], path[(i + hop) % ring]) for i in range(ring)],
            )
            running = running + got.astype(f32)
        value = running * depth ** (-0.5)
        rewards.append(
            jnp.sum(value * jax.nn.sigmoid(value) * head[:, begin * tile : end * tile], axis=1)
        )
    partial = sum(rewards)
    each = partial.shape[0] // group
    result = partial[:each]
    for k in range(1, group):
        result = result + across(partial[k * each : (k + 1) * each], k)
    return (momentum_out, result * hidden_units ** (-0.5))


def solution(mesh):
    replicas, group = mesh.shape["replica"], mesh.shape["fsdp"]
    chips = Mesh(mesh.devices.reshape(replicas // 2, 2, group), ("ring", "core", "fsdp"))

    return jax.shard_map(
        shards,
        mesh=chips,
        in_specs=(
            P(None, "fsdp"),
            P("fsdp"),
            P(("ring", "core"), "fsdp"),
            P(None, ("ring", "core", "fsdp"), None),
            P(None, ("ring", "core"), None),
            P(("ring", "core", "fsdp"), None),
        ),
        out_specs=(P(("ring", "core"), "fsdp"), P(("ring", "core", "fsdp"))),
        check_vma=False,
    )
```

```python
import functools

import jax
import jax.numpy as jnp
from jax import lax
from jax.experimental import pallas as pl
from jax.experimental.pallas import tpu as pltpu
from jax.sharding import Mesh
from jax.sharding import PartitionSpec as P


BLOCK = 128

inner_rate = 300.0
outer_rate = 0.7
outer_decay = 0.9
code_top = 448.0
epsilon = 1e-06

f32 = jnp.float32
bf16 = jnp.bfloat16


def tile_of(extent, top):
    tile = top
    while extent % tile:
        tile //= 2
    return tile


def whole(shape):
    return pl.BlockSpec(shape, lambda *_: (0,) * len(shape))


def params(mib=40):
    return pltpu.CompilerParams(
        dimension_semantics=("arbitrary",), vmem_limit_bytes=mib << 20
    )


def forward_kernel(places, scale, unit_scale, own_rows, first, last, where, *refs):
    blocks = refs[: len(places)]
    w, head = refs[len(places) : len(places) + 2]
    refs = refs[len(places) + 2 :]
    if not first:
        prior = refs[0]
        refs = refs[2:]
    slope, partial = refs[:2]
    refs = refs[2:]
    if first:
        mine_t, other_t = refs[:2]
        refs = refs[2:]
    rows, sums = refs

    @pl.when(pl.program_id(0) == 0)
    def _():
        for (start, size), block in zip(places, blocks):
            rows[start : start + size, :] = block[...]
        sums[...] = jnp.zeros_like(sums) if first else prior[...]
        if first:
            for place, out in ((0, mine_t), (1, other_t)):
                begin = pl.multiple_of(where[place] * own_rows, 128)
                out[...] = rows[:, pl.ds(begin, own_rows)].T

    width = min(256, w.shape[1])
    for start in range(0, w.shape[1], width):
        value = jnp.dot(rows[...], w[:, start : start + width], preferred_element_type=f32) * scale
        weight = head[:, start : start + width]
        squash = jax.nn.sigmoid(value)
        slope[:, start : start + width] = (
            weight * unit_scale * squash * (1.0 + value * (1.0 - squash))
        )
        term = value * squash * weight
        total = sums[...]
        for lane in range(0, width, 128):
            total = total + term[:, lane : lane + 128]
        sums[...] = total

    @pl.when(pl.program_id(0) == pl.num_programs(0) - 1)
    def _():
        if last:
            column = jnp.sum(sums[...], axis=1, keepdims=True)
            partial[...] = jnp.broadcast_to(column, sums.shape).T[0:1, :]
        else:
            partial[...] = sums[...]


def places_of(blocks):
    places = []
    for item in blocks:
        places.append((sum(size for _, size in places), item.shape[0]))
    return places


def cut_kernel(places, where, *refs):
    for (start, size), block in zip(places, refs):
        refs[-1][start : start + size, :] = block[...]


def cut_call(where, blocks, width):
    places = places_of(blocks)
    count = sum(size for _, size in places)
    return pl.pallas_call(
        functools.partial(cut_kernel, places),
        out_shape=jax.ShapeDtypeStruct((count, width), bf16),
        grid_spec=pltpu.PrefetchScalarGridSpec(
            num_scalar_prefetch=1,
            grid=(1,),
            in_specs=[
                pl.BlockSpec((size, width), lambda j, where: (0, where[2])) for _, size in places
            ],
            out_specs=whole((count, width)),
        ),
        compiler_params=params(8),
        cost_estimate=pl.CostEstimate(flops=0, bytes_accessed=4 * count * width, transcendentals=0),
    )(where, *blocks)


def join_kernel(places, *refs):
    for (start, size), item in zip(places, refs):
        refs[-1][:, start : start + size] = item[...]


def join_call(items):
    places, start = [], 0
    for item in items:
        places.append((start, item.shape[1]))
        start += item.shape[1]
    shape = (items[0].shape[0], start)
    return pl.pallas_call(
        functools.partial(join_kernel, places),
        out_shape=jax.ShapeDtypeStruct(shape, bf16),
        grid=(1,),
        in_specs=[whole(item.shape) for item in items],
        out_specs=whole(shape),
        compiler_params=params(16),
        cost_estimate=pl.CostEstimate(
            flops=0, bytes_accessed=4 * shape[0] * shape[1], transcendentals=0
        ),
    )(*items)


def turn_kernel(where, mine, other, mine_t, other_t):
    mine_t[...] = mine[...].T
    other_t[...] = other[...].T


def turn_call(where, piece):
    count, width = piece.shape[0], piece.shape[1] // 2
    return pl.pallas_call(
        turn_kernel,
        out_shape=[jax.ShapeDtypeStruct((width, count), bf16)] * 2,
        grid_spec=pltpu.PrefetchScalarGridSpec(
            num_scalar_prefetch=1,
            grid=(1,),
            in_specs=[
                pl.BlockSpec((count, width), lambda j, where: (0, where[3])),
                pl.BlockSpec((count, width), lambda j, where: (0, where[4])),
            ],
            out_specs=[whole((width, count))] * 2,
        ),
        compiler_params=params(8),
        cost_estimate=pl.CostEstimate(flops=0, bytes_accessed=8 * count * width, transcendentals=0),
    )(where, piece, piece)


def forward_call(
    where, blocks, places, weights, head, hidden_units, own_rows, tile, begin, end, prior, slope
):
    depth, columns = weights.shape
    last = end * tile == columns
    count = sum(size for _, size in places)
    width = (end - begin) * tile
    first = prior is None
    turned = (own_rows, count)
    sums = (1, count) if last else (count, 128)
    n_blocks = len(blocks)
    return pl.pallas_call(
        functools.partial(
            forward_kernel, places, depth ** (-0.5), hidden_units ** (-0.5), own_rows, first, last
        ),
        out_shape=[
            jax.ShapeDtypeStruct((count, columns), f32),
            jax.ShapeDtypeStruct(sums, f32),
        ]
        + [jax.ShapeDtypeStruct(turned, bf16)] * (2 if first else 0),
        grid_spec=pltpu.PrefetchScalarGridSpec(
            num_scalar_prefetch=1,
            grid=(end - begin,),
            in_specs=[whole(block.shape) for block in blocks]
            + [
                pl.BlockSpec((depth, tile), lambda j, *_: (0, begin + j)),
                pl.BlockSpec((1, tile), lambda j, *_: (0, begin + j)),
            ]
            + ([] if first else [whole((count, 128)), pl.BlockSpec(memory_space=pl.ANY)]),
            out_specs=[
                pl.BlockSpec((count, tile), lambda j, *_: (0, begin + j)),
                whole(sums),
            ]
            + [whole(turned)] * (2 if first else 0),
            scratch_shapes=[
                pltpu.VMEM((count, depth), bf16),
                pltpu.VMEM((count, 128), f32),
            ],
        ),
        input_output_aliases={} if first else {n_blocks + 4: 0},
        compiler_params=params(30),
        cost_estimate=pl.CostEstimate(
            flops=2 * count * depth * width,
            bytes_accessed=2 * depth * width + 4 * count * width,
            transcendentals=count * width,
        ),
    )(where, *blocks, weights, head, *(() if first else (prior, slope)))


def grad_kernel(group, scale, replicas, *refs):
    pairs = refs[:replicas]
    partials = refs[replicas : replicas + group]
    slope, out, reward_grad = refs[replicas + group :]

    @pl.when(pl.program_id(0) == 0)
    def _():
        n_pairs = pairs[0].shape[1]
        rows = reward_grad.shape[0] // len(pairs)
        size = rows // group
        columns = [
            jnp.broadcast_to(partial[...], (n_pairs, reward_grad.shape[0])).T for partial in partials
        ]
        for at, pair in enumerate(pairs):
            rewards = jnp.zeros((rows, n_pairs), f32)
            for k, column in enumerate(columns):
                starts = [at * rows + (j ^ k) * size for j in range(group)]
                rewards = rewards + jnp.concatenate([column[b : b + size] for b in starts], axis=0)
            rewards = rewards * scale
            position = lax.broadcasted_iota(jnp.int32, (rows, n_pairs), 0)
            table = (position == pair[1:2, :]).astype(f32) - (position == pair[0:1, :]).astype(f32)
            gap = jnp.sum(table * rewards, axis=0, keepdims=True)
            pair_weight = jax.nn.sigmoid(gap)
            column = jnp.sum(table * pair_weight, axis=1, keepdims=True)
            reward_grad[at * rows : (at + 1) * rows, :] = jnp.broadcast_to(column, (rows, 128))

    out[...] = (reward_grad[:, 0:1] * slope[...]).astype(bf16)


def grad_call(pairs, partials, slope, hidden_units, tile, begin, end):
    rows = slope.shape[0]
    mib = 20
    columns = (end - begin) * tile
    offset = 0
    if begin == 0 and end % 2 == 1 and (end * tile) % 256 == 0 and columns == slope.shape[1]:
        tile = columns // 2
    elif begin % (end - begin) == 0:
        offset, tile = begin // (end - begin), columns
    else:
        offset = begin
    return pl.pallas_call(
        functools.partial(grad_kernel, len(partials), hidden_units ** (-0.5), len(pairs)),
        out_shape=jax.ShapeDtypeStruct((rows, columns), bf16),
        grid=(columns // tile,),
        in_specs=[whole(pair.shape) for pair in pairs]
        + [whole(partial.shape) for partial in partials]
        + [pl.BlockSpec((rows, tile), lambda j: (0, offset + j))],
        out_specs=pl.BlockSpec((rows, tile), lambda j: (0, j)),
        scratch_shapes=[pltpu.VMEM((rows, 128), f32)],
        compiler_params=params(mib),
        cost_estimate=pl.CostEstimate(
            flops=2 * rows * columns, bytes_accessed=6 * rows * columns, transcendentals=0
        ),
    )(*pairs, *partials, slope)


def coded_sum(x_t, grads, span, start, factor):
    raws, column = [], 0
    for grad in grads:
        for at in range(0, grad.shape[0], span):
            rows = x_t[start : start + BLOCK, column : column + span]
            raws.append(jnp.dot(rows, grad[at : at + span, :], preferred_element_type=f32))
            column += span
    largest = jnp.concatenate(
        [jnp.max(jnp.abs(raw), axis=0, keepdims=True) for raw in raws], axis=0
    )
    scale = ((largest * factor + epsilon) / code_top).astype(bf16).astype(f32)
    inverse = factor / scale
    total = None
    for k, raw in enumerate(raws):
        coded = (raw * inverse[k : k + 1]).astype(bf16)
        decoded = coded.astype(f32) * scale[k : k + 1]
        total = decoded if total is None else total + decoded
    return total


def settle_kernel(chained, n_grads, span, factor, replicas, order, where, *refs):
    if chained:
        refs = refs[1:]
    x_t, grads = refs[0], refs[1 : 1 + n_grads]
    momentum, w, rows, momentum_out, near, far, sorted_rows, new_w = refs[1 + n_grads :]
    slots = order.shape[0]
    size = rows.shape[0] // slots

    @pl.when(pl.program_id(0) == 0)
    def _():
        for slot in range(slots):
            begin = pl.multiple_of(order[slot] * size, size)
            sorted_rows[slot * size : (slot + 1) * size, :] = rows[pl.ds(begin, size), :]

    updates = []
    for start in range(0, momentum.shape[0], BLOCK):
        part = slice(start, start + BLOCK)
        pseudo = coded_sum(x_t, grads, span, start, factor) * (1.0 / replicas)
        moved = outer_decay * momentum[part, :] + pseudo
        momentum_out[part, :] = moved
        updates.append(outer_rate * (pseudo + outer_decay * moved))
    largest = jnp.concatenate(
        [jnp.max(jnp.abs(update), axis=0, keepdims=True) for update in updates], axis=0
    )
    scale = ((largest + epsilon) / code_top).astype(bf16).astype(f32)
    inverse = 1.0 / scale
    for k, update in enumerate(updates):
        part = slice(k * BLOCK, (k + 1) * BLOCK)
        coded = (update * inverse[k : k + 1]).astype(bf16)
        decoded = coded.astype(f32) * scale[k : k + 1]
        new_w[part, :] = (w[part, :].astype(f32) - decoded).astype(bf16)
    value = jnp.dot(sorted_rows[...], new_w[...], preferred_element_type=f32)
    half = value.shape[0] // 2
    near[...] = value[:half]
    far[...] = value[half:]


def settle_call(
    chain, order, where, x_t, terms, momentum, weights, rows, span, factor, replicas, tile, begin, end
):
    own_rows, columns = momentum.shape
    width = (end - begin) * tile
    chained = chain is not None
    local = lambda j, *_: (0, j)
    down = lambda j, *_: (0, begin + j)
    out_rows = rows.shape[0] // 2
    term_specs = [whole(x_t.shape)]
    for grad, start in terms:
        place = lambda j, *_, start=start: (0, start + j)
        term_specs.append(pl.BlockSpec((grad.shape[0], tile), place))
    depth = x_t.shape[1]
    return pl.pallas_call(
        functools.partial(settle_kernel, chained, len(terms), span, factor, replicas),
        out_shape=(
            jax.ShapeDtypeStruct((own_rows, columns), f32),
            jax.ShapeDtypeStruct((out_rows, width), f32),
            jax.ShapeDtypeStruct((out_rows, width), f32),
        ),
        grid_spec=pltpu.PrefetchScalarGridSpec(
            num_scalar_prefetch=2,
            grid=(end - begin,),
            in_specs=([pl.BlockSpec(memory_space=pl.ANY)] if chained else [])
            + term_specs
            + [
                pl.BlockSpec((own_rows, tile), down),
                pl.BlockSpec((own_rows, tile), lambda j, order, where: (where[0], begin + j)),
                whole(rows.shape),
            ],
            out_specs=[
                pl.BlockSpec((own_rows, tile), down),
                pl.BlockSpec((out_rows, tile), local),
                pl.BlockSpec((out_rows, tile), local),
            ],
            scratch_shapes=[
                pltpu.VMEM(rows.shape, bf16),
                pltpu.VMEM((own_rows, tile), bf16),
            ],
        ),
        input_output_aliases={2: 0} if chained else {},
        compiler_params=params(40),
        cost_estimate=pl.CostEstimate(
            flops=(2 * own_rows * depth + 2 * own_rows * rows.shape[0]) * width,
            bytes_accessed=(10 * own_rows + 2 * depth + 4 * rows.shape[0]) * width,
            transcendentals=0,
        ),
    )(
        order, where, *((chain,) if chained else ()), x_t, *(grad for grad, _ in terms),
        momentum, weights, rows,
    )


def shards(weights, head_vector, momentum, batches, pair_index, eval_rows):
    ring, group = lax.axis_size("ring"), lax.axis_size("fsdp")
    replicas = 2 * ring
    depth, columns = weights.shape
    hidden_units = columns * group
    own_rows = momentum.shape[0]
    block = batches.shape[1]
    span = block * group
    at_ring, at_core, at_fsdp = (lax.axis_index(name) for name in ("ring", "core", "fsdp"))
    path = list(range(0, 1)) + list(range(1, ring, 2)) + list(range(2, ring, 2))[::-1]
    onward = [(path[i], path[(i + 1) % ring]) for i in range(ring)]
    at_spot = jnp.where(at_ring % 2 == 1, (at_ring + 1) // 2, (ring - at_ring // 2) % ring)

    def chip_at(spot):
        return jnp.where(spot == 0, 0, jnp.where(spot <= ring // 2, 2 * spot - 1, 2 * (ring - spot)))

    tile = tile_of(columns, 512)
    tiles = columns // tile
    first = (5 * tiles + 6) // 7
    outer_cuts = [cut for cut in ((0, first), (first, tiles)) if cut[0] < cut[1]]

    def along(value):
        return lax.ppermute(value, "ring", onward)

    def across(value, k):
        return lax.ppermute(value, "fsdp", [(i, i ^ k) for i in range(group)])

    def back(value):
        return lax.ppermute(value, "ring", [(b, a) for a, b in onward])

    def swap(value):
        return lax.ppermute(value, "core", [(0, 1), (1, 0)])

    replica = at_ring * 2 + at_core
    before = chip_at((at_spot - 1) % ring)
    where = jnp.stack([replica, at_ring * 2 + 1 - at_core, before, at_core, 1 - at_core]).astype(jnp.int32)
    head = head_vector.reshape(1, columns)

    pairs = pair_index[0].T
    pairs = [((pairs // block) ^ at_fsdp) * block + pairs % block]
    for hop in range(1, ring - 1):
        pairs.append(
            lax.ppermute(pairs[0], "ring", [(path[i], path[(i + hop) % ring]) for i in range(ring)])
        )

    half = block // 2
    steps = []
    own = batches[0]
    for step in range(ring - 1):
        if step:
            own = along(own)
        if group != 4:
            steps.append([own] + [across(own, k) for k in range(1, group)])
        elif step == 0:
            up, low = own[:half], own[half:]
            one = [across(up, 1), across(low, 1)]
            two = [across(up, 2), across(low, 2)]
            last = [across(one[0], 2), across(two[1], 1)]
            steps.append([own] + one + two + last)
        else:
            sides = [across(own, 1), across(own, 2)]
            if step == 1:
                last = [along(steps[0][-2]), along(steps[0][-1])]
            else:
                last = [across(own, 3)]
            steps.append([own] + sides + last)

    shares = [eval_rows] + [across(eval_rows, k) for k in range(1, group)]
    rows = lax.all_to_all(
        jnp.concatenate(shares, axis=0), ("ring", "core"), split_axis=1, concat_axis=0, tiled=True
    )
    order = chip_at((at_spot - 1 - jnp.arange(ring, dtype=jnp.int32)) % ring)
    order = jnp.concatenate([order * 2 + at_core, order * 2 + 1 - at_core]).astype(jnp.int32)
    where, order = lax.optimization_barrier((where, order))


    factor = inner_rate * depth ** (-0.5)
    terms = []
    piece = cut_call(where, steps[0], 2 * own_rows)
    piece = back(piece)
    next_t, next_other_t = turn_call(where, piece)
    chunks = [[0]] + [[step, step + 1] for step in range(1, ring - 1, 2)]
    for chunk in chunks:
        name = chunk[0]
        blocks = [item for step in chunk for item in steps[step]]
        places = places_of(blocks)
        slope = partial = None
        for begin, end in [(0, tiles)]:
            outs = forward_call(
                where, blocks, places, weights, head, hidden_units, own_rows, tile, begin, end,
                partial, slope,
            )
            slope, partial = outs[:2]
            if begin == 0:
                mine_t, other_t = outs[2:]
        partials = [partial] + [across(partial, k) for k in range(1, group)]
        other_t = swap(other_t)
        chunk_pairs = [pairs[step] for step in chunk]
        part_cuts = outer_cuts if name == 0 or chunk is chunks[-1] else [(0, tiles)]
        mine_parts, other_parts = [], []
        for begin, end in part_cuts:
            part = grad_call(chunk_pairs, partials, slope, hidden_units, tile, begin, end)
            mine_parts.append((part, begin))
            other_parts.append((swap(part), begin))
        terms += [(mine_t, mine_parts), (other_t, other_parts)]
        if name == 0:
            next_parts = [(back(part), begin) for part, begin in mine_parts]
    swapped_parts = [(swap(part), begin) for part, begin in next_parts]
    terms += [(next_t, next_parts), (swap(next_other_t), swapped_parts)]

    x_t = join_call([item for item, _ in terms])
    momentum_out = None
    rewards = []
    share = rows.shape[0] // replicas
    for begin, end in outer_cuts:
        part_terms = []
        for _, parts in terms:
            grad, start = [part for part in parts if part[1] <= begin][-1]
            part_terms.append((grad, begin - start))
        momentum_out, near, far = settle_call(
            momentum_out, order, where, x_t, part_terms, momentum, weights, rows, span, factor, replicas,
            tile, begin, end,
        )
        far = swap(far)
        running = near[-share:] + far[-share:]
        for hop in range(1, ring):
            piece = slice((ring - 1 - hop) * share, (ring - hop) * share)
            got = lax.ppermute(
                (near[piece] + far[piece]).astype(bf16),
                "ring",
                [(path[i], path[(i + hop) % ring]) for i in range(ring)],
            )
            running = running + got.astype(f32)
        value = running * depth ** (-0.5)
        rewards.append(
            jnp.sum(value * jax.nn.sigmoid(value) * head[:, begin * tile : end * tile], axis=1)
        )
    partial = sum(rewards)
    each = partial.shape[0] // group
    result = partial[:each]
    for k in range(1, group):
        result = result + across(partial[k * each : (k + 1) * each], k)
    return (momentum_out, result * hidden_units ** (-0.5))


def solution(mesh):
    replicas, group = mesh.shape["replica"], mesh.shape["fsdp"]
    chips = Mesh(mesh.devices.reshape(replicas // 2, 2, group), ("ring", "core", "fsdp"))

    return jax.shard_map(
        shards,
        mesh=chips,
        in_specs=(
            P(None, "fsdp"),
            P("fsdp"),
            P(("ring", "core"), "fsdp"),
            P(None, ("ring", "core", "fsdp"), None),
            P(None, ("ring", "core"), None),
            P(("ring", "core", "fsdp"), None),
        ),
        out_specs=(P(("ring", "core"), "fsdp"), P(("ring", "core", "fsdp"))),
        check_vma=False,
    )
```

```python
import functools

import jax
import jax.numpy as jnp
from jax import lax
from jax.experimental import pallas as pl
from jax.experimental.pallas import tpu as pltpu
from jax.sharding import Mesh
from jax.sharding import PartitionSpec as P


BLOCK = 128

inner_rate = 300.0
outer_rate = 0.7
outer_decay = 0.9
code_top = 448.0
epsilon = 1e-06

f32 = jnp.float32
bf16 = jnp.bfloat16


def tile_of(extent, top):
    tile = top
    while extent % tile:
        tile //= 2
    return tile


def whole(shape):
    return pl.BlockSpec(shape, lambda *_: (0,) * len(shape))


def params(mib=40):
    return pltpu.CompilerParams(
        dimension_semantics=("arbitrary",), vmem_limit_bytes=mib << 20
    )


def forward_kernel(places, scale, unit_scale, own_rows, first, last, where, *refs):
    blocks = refs[: len(places)]
    w, head = refs[len(places) : len(places) + 2]
    refs = refs[len(places) + 2 :]
    if not first:
        prior = refs[0]
        refs = refs[2:]
    slope, partial = refs[:2]
    refs = refs[2:]
    if first:
        mine_t, other_t = refs[:2]
        refs = refs[2:]
    rows, sums = refs

    @pl.when(pl.program_id(0) == 0)
    def _():
        for (start, size), block in zip(places, blocks):
            rows[start : start + size, :] = block[...]
        sums[...] = jnp.zeros_like(sums) if first else prior[...]
        if first:
            for place, out in ((0, mine_t), (1, other_t)):
                begin = pl.multiple_of(where[place] * own_rows, 128)
                out[...] = rows[:, pl.ds(begin, own_rows)].T

    width = min(256, w.shape[1])
    for start in range(0, w.shape[1], width):
        value = jnp.dot(rows[...], w[:, start : start + width], preferred_element_type=f32) * scale
        weight = head[:, start : start + width]
        squash = jax.nn.sigmoid(value)
        slope[:, start : start + width] = (
            weight * unit_scale * squash * (1.0 + value * (1.0 - squash))
        )
        term = value * squash * weight
        total = sums[...]
        for lane in range(0, width, 128):
            total = total + term[:, lane : lane + 128]
        sums[...] = total

    @pl.when(pl.program_id(0) == pl.num_programs(0) - 1)
    def _():
        if last:
            column = jnp.sum(sums[...], axis=1, keepdims=True)
            partial[...] = jnp.broadcast_to(column, sums.shape).T[0:1, :]
        else:
            partial[...] = sums[...]


def places_of(blocks):
    places = []
    for item in blocks:
        places.append((sum(size for _, size in places), item.shape[0]))
    return places


def cut_kernel(places, corner, where, *refs):
    inputs = len(places) + len(corner)
    for (start, size), block in zip(places, refs):
        refs[inputs][start : start + size, :] = block[...]
    for (start, size), block in zip(corner, refs[len(places) : inputs]):
        refs[-1][start : start + size, :] = block[...]


def cut_call(where, blocks, width, joined):
    places, corner = places_of(blocks), places_of(joined)
    count = sum(size for _, size in places)
    depth = blocks[0].shape[1]
    shapes = [(count, width)] + ([(sum(size for _, size in corner), depth)] if joined else [])
    return pl.pallas_call(
        functools.partial(cut_kernel, places, corner),
        out_shape=[jax.ShapeDtypeStruct(shape, bf16) for shape in shapes],
        grid_spec=pltpu.PrefetchScalarGridSpec(
            num_scalar_prefetch=1,
            grid=(1,),
            in_specs=[
                pl.BlockSpec((size, width), lambda j, where: (0, where[2])) for _, size in places
            ]
            + [whole(item.shape) for item in joined],
            out_specs=[whole(shape) for shape in shapes],
        ),
        compiler_params=params(8),
        cost_estimate=pl.CostEstimate(flops=0, bytes_accessed=4 * count * width, transcendentals=0),
    )(where, *blocks, *joined)


def join_kernel(places, *refs):
    for (start, size), item in zip(places, refs):
        refs[-1][:, start : start + size] = item[...]


def join_call(items):
    places, start = [], 0
    for item in items:
        places.append((start, item.shape[1]))
        start += item.shape[1]
    shape = (items[0].shape[0], start)
    return pl.pallas_call(
        functools.partial(join_kernel, places),
        out_shape=jax.ShapeDtypeStruct(shape, bf16),
        grid=(1,),
        in_specs=[whole(item.shape) for item in items],
        out_specs=whole(shape),
        compiler_params=params(16),
        cost_estimate=pl.CostEstimate(
            flops=0, bytes_accessed=4 * shape[0] * shape[1], transcendentals=0
        ),
    )(*items)


def turn_kernel(where, mine, other, mine_t, other_t):
    mine_t[...] = mine[...].T
    other_t[...] = other[...].T


def turn_call(where, piece):
    count, width = piece.shape[0], piece.shape[1] // 2
    return pl.pallas_call(
        turn_kernel,
        out_shape=[jax.ShapeDtypeStruct((width, count), bf16)] * 2,
        grid_spec=pltpu.PrefetchScalarGridSpec(
            num_scalar_prefetch=1,
            grid=(1,),
            in_specs=[
                pl.BlockSpec((count, width), lambda j, where: (0, where[3])),
                pl.BlockSpec((count, width), lambda j, where: (0, where[4])),
            ],
            out_specs=[whole((width, count))] * 2,
        ),
        compiler_params=params(8),
        cost_estimate=pl.CostEstimate(flops=0, bytes_accessed=8 * count * width, transcendentals=0),
    )(where, piece, piece)


def forward_call(
    where, blocks, places, weights, head, hidden_units, own_rows, tile, begin, end, prior, slope
):
    depth, columns = weights.shape
    last = end * tile == columns
    count = sum(size for _, size in places)
    width = (end - begin) * tile
    first = prior is None
    turned = (own_rows, count)
    sums = (1, count) if last else (count, 128)
    n_blocks = len(blocks)
    return pl.pallas_call(
        functools.partial(
            forward_kernel, places, depth ** (-0.5), hidden_units ** (-0.5), own_rows, first, last
        ),
        out_shape=[
            jax.ShapeDtypeStruct((count, columns), f32),
            jax.ShapeDtypeStruct(sums, f32),
        ]
        + [jax.ShapeDtypeStruct(turned, bf16)] * (2 if first else 0),
        grid_spec=pltpu.PrefetchScalarGridSpec(
            num_scalar_prefetch=1,
            grid=(end - begin,),
            in_specs=[whole(block.shape) for block in blocks]
            + [
                pl.BlockSpec((depth, tile), lambda j, *_: (0, begin + j)),
                pl.BlockSpec((1, tile), lambda j, *_: (0, begin + j)),
            ]
            + ([] if first else [whole((count, 128)), pl.BlockSpec(memory_space=pl.ANY)]),
            out_specs=[
                pl.BlockSpec((count, tile), lambda j, *_: (0, begin + j)),
                whole(sums),
            ]
            + [whole(turned)] * (2 if first else 0),
            scratch_shapes=[
                pltpu.VMEM((count, depth), bf16),
                pltpu.VMEM((count, 128), f32),
            ],
        ),
        input_output_aliases={} if first else {n_blocks + 4: 0},
        compiler_params=params(30),
        cost_estimate=pl.CostEstimate(
            flops=2 * count * depth * width,
            bytes_accessed=2 * depth * width + 4 * count * width,
            transcendentals=count * width,
        ),
    )(where, *blocks, weights, head, *(() if first else (prior, slope)))


def grad_kernel(group, scale, replicas, *refs):
    pairs = refs[:replicas]
    partials = refs[replicas : replicas + group]
    slope, out, reward_grad = refs[replicas + group :]

    @pl.when(pl.program_id(0) == 0)
    def _():
        n_pairs = pairs[0].shape[1]
        rows = reward_grad.shape[0] // len(pairs)
        size = rows // group
        columns = [
            jnp.broadcast_to(partial[...], (n_pairs, reward_grad.shape[0])).T for partial in partials
        ]
        for at, pair in enumerate(pairs):
            rewards = jnp.zeros((rows, n_pairs), f32)
            for k, column in enumerate(columns):
                starts = [at * rows + (j ^ k) * size for j in range(group)]
                rewards = rewards + jnp.concatenate([column[b : b + size] for b in starts], axis=0)
            rewards = rewards * scale
            position = lax.broadcasted_iota(jnp.int32, (rows, n_pairs), 0)
            table = (position == pair[1:2, :]).astype(f32) - (position == pair[0:1, :]).astype(f32)
            gap = jnp.sum(table * rewards, axis=0, keepdims=True)
            pair_weight = jax.nn.sigmoid(gap)
            column = jnp.sum(table * pair_weight, axis=1, keepdims=True)
            reward_grad[at * rows : (at + 1) * rows, :] = jnp.broadcast_to(column, (rows, 128))

    out[...] = (reward_grad[:, 0:1] * slope[...]).astype(bf16)


def grad_call(pairs, partials, slope, hidden_units, tile, begin, end):
    rows = slope.shape[0]
    mib = 20
    columns = (end - begin) * tile
    offset = 0
    if begin == 0 and end % 2 == 1 and (end * tile) % 256 == 0 and columns == slope.shape[1]:
        tile = columns // 2
    elif begin % (end - begin) == 0:
        offset, tile = begin // (end - begin), columns
    else:
        offset = begin
    return pl.pallas_call(
        functools.partial(grad_kernel, len(partials), hidden_units ** (-0.5), len(pairs)),
        out_shape=jax.ShapeDtypeStruct((rows, columns), bf16),
        grid=(columns // tile,),
        in_specs=[whole(pair.shape) for pair in pairs]
        + [whole(partial.shape) for partial in partials]
        + [pl.BlockSpec((rows, tile), lambda j: (0, offset + j))],
        out_specs=pl.BlockSpec((rows, tile), lambda j: (0, j)),
        scratch_shapes=[pltpu.VMEM((rows, 128), f32)],
        compiler_params=params(mib),
        cost_estimate=pl.CostEstimate(
            flops=2 * rows * columns, bytes_accessed=6 * rows * columns, transcendentals=0
        ),
    )(*pairs, *partials, slope)


def coded_sum(x_t, grads, span, start, factor):
    raws, column = [], 0
    for grad in grads:
        for at in range(0, grad.shape[0], span):
            rows = x_t[start : start + BLOCK, column : column + span]
            raws.append(jnp.dot(rows, grad[at : at + span, :], preferred_element_type=f32))
            column += span
    largest = jnp.concatenate(
        [jnp.max(jnp.abs(raw), axis=0, keepdims=True) for raw in raws], axis=0
    )
    scale = ((largest * factor + epsilon) / code_top).astype(bf16).astype(f32)
    inverse = factor / scale
    total = None
    for k, raw in enumerate(raws):
        coded = (raw * inverse[k : k + 1]).astype(bf16)
        decoded = coded.astype(f32) * scale[k : k + 1]
        total = decoded if total is None else total + decoded
    return total


def settle_kernel(chained, n_grads, span, factor, replicas, order, where, *refs):
    if chained:
        refs = refs[1:]
    x_t, grads = refs[0], refs[1 : 1 + n_grads]
    momentum, w, rows, momentum_out, near, far, sorted_rows, new_w = refs[1 + n_grads :]
    slots = order.shape[0]
    size = rows.shape[0] // slots

    @pl.when(pl.program_id(0) == 0)
    def _():
        for slot in range(slots):
            begin = pl.multiple_of(order[slot] * size, size)
            sorted_rows[slot * size : (slot + 1) * size, :] = rows[pl.ds(begin, size), :]

    updates = []
    for start in range(0, momentum.shape[0], BLOCK):
        part = slice(start, start + BLOCK)
        pseudo = coded_sum(x_t, grads, span, start, factor) * (1.0 / replicas)
        moved = outer_decay * momentum[part, :] + pseudo
        momentum_out[part, :] = moved
        updates.append(outer_rate * (pseudo + outer_decay * moved))
    largest = jnp.concatenate(
        [jnp.max(jnp.abs(update), axis=0, keepdims=True) for update in updates], axis=0
    )
    scale = ((largest + epsilon) / code_top).astype(bf16).astype(f32)
    inverse = 1.0 / scale
    for k, update in enumerate(updates):
        part = slice(k * BLOCK, (k + 1) * BLOCK)
        coded = (update * inverse[k : k + 1]).astype(bf16)
        decoded = coded.astype(f32) * scale[k : k + 1]
        new_w[part, :] = (w[part, :].astype(f32) - decoded).astype(bf16)
    value = jnp.dot(sorted_rows[...], new_w[...], preferred_element_type=f32)
    half = value.shape[0] // 2
    near[...] = value[:half]
    far[...] = value[half:]


def settle_call(
    chain, order, where, x_t, terms, momentum, weights, rows, span, factor, replicas, tile, begin, end
):
    own_rows, columns = momentum.shape
    width = (end - begin) * tile
    chained = chain is not None
    local = lambda j, *_: (0, j)
    down = lambda j, *_: (0, begin + j)
    out_rows = rows.shape[0] // 2
    term_specs = [whole(x_t.shape)]
    for grad, start in terms:
        place = lambda j, *_, start=start: (0, start + j)
        term_specs.append(pl.BlockSpec((grad.shape[0], tile), place))
    depth = x_t.shape[1]
    return pl.pallas_call(
        functools.partial(settle_kernel, chained, len(terms), span, factor, replicas),
        out_shape=(
            jax.ShapeDtypeStruct((own_rows, columns), f32),
            jax.ShapeDtypeStruct((out_rows, width), f32),
            jax.ShapeDtypeStruct((out_rows, width), f32),
        ),
        grid_spec=pltpu.PrefetchScalarGridSpec(
            num_scalar_prefetch=2,
            grid=(end - begin,),
            in_specs=([pl.BlockSpec(memory_space=pl.ANY)] if chained else [])
            + term_specs
            + [
                pl.BlockSpec((own_rows, tile), down),
                pl.BlockSpec((own_rows, tile), lambda j, order, where: (where[0], begin + j)),
                whole(rows.shape),
            ],
            out_specs=[
                pl.BlockSpec((own_rows, tile), down),
                pl.BlockSpec((out_rows, tile), local),
                pl.BlockSpec((out_rows, tile), local),
            ],
            scratch_shapes=[
                pltpu.VMEM(rows.shape, bf16),
                pltpu.VMEM((own_rows, tile), bf16),
            ],
        ),
        input_output_aliases={2: 0} if chained else {},
        compiler_params=params(40),
        cost_estimate=pl.CostEstimate(
            flops=(2 * own_rows * depth + 2 * own_rows * rows.shape[0]) * width,
            bytes_accessed=(10 * own_rows + 2 * depth + 4 * rows.shape[0]) * width,
            transcendentals=0,
        ),
    )(
        order, where, *((chain,) if chained else ()), x_t, *(grad for grad, _ in terms),
        momentum, weights, rows,
    )


def shards(weights, head_vector, momentum, batches, pair_index, eval_rows):
    ring, group = lax.axis_size("ring"), lax.axis_size("fsdp")
    replicas = 2 * ring
    depth, columns = weights.shape
    hidden_units = columns * group
    own_rows = momentum.shape[0]
    block = batches.shape[1]
    span = block * group
    at_ring, at_core, at_fsdp = (lax.axis_index(name) for name in ("ring", "core", "fsdp"))
    path = list(range(0, 1)) + list(range(1, ring, 2)) + list(range(2, ring, 2))[::-1]
    onward = [(path[i], path[(i + 1) % ring]) for i in range(ring)]
    at_spot = jnp.where(at_ring % 2 == 1, (at_ring + 1) // 2, (ring - at_ring // 2) % ring)

    def chip_at(spot):
        return jnp.where(spot == 0, 0, jnp.where(spot <= ring // 2, 2 * spot - 1, 2 * (ring - spot)))

    tile = tile_of(columns, 512)
    tiles = columns // tile
    first = (5 * tiles + 6) // 7
    outer_cuts = [cut for cut in ((0, first), (first, tiles)) if cut[0] < cut[1]]

    def along(value):
        return lax.ppermute(value, "ring", onward)

    def across(value, k):
        return lax.ppermute(value, "fsdp", [(i, i ^ k) for i in range(group)])

    def back(value):
        return lax.ppermute(value, "ring", [(b, a) for a, b in onward])

    def swap(value):
        return lax.ppermute(value, "core", [(0, 1), (1, 0)])

    replica = at_ring * 2 + at_core
    before = chip_at((at_spot - 1) % ring)
    where = jnp.stack([replica, at_ring * 2 + 1 - at_core, before, at_core, 1 - at_core]).astype(jnp.int32)
    head = head_vector.reshape(1, columns)

    pairs = pair_index[0].T
    pairs = [((pairs // block) ^ at_fsdp) * block + pairs % block]
    for hop in range(1, ring - 1):
        pairs.append(
            lax.ppermute(pairs[0], "ring", [(path[i], path[(i + hop) % ring]) for i in range(ring)])
        )

    half = block // 2
    steps = []
    own = batches[0]
    for step in range(ring - 1):
        if step:
            own = along(own)
        if group != 4:
            steps.append([own] + [across(own, k) for k in range(1, group)])
        elif step == 0:
            up, low = own[:half], own[half:]
            one = [across(up, 1), across(low, 1)]
            two = [across(up, 2), across(low, 2)]
            last = [across(one[0], 2), across(two[1], 1)]
            steps.append([own] + one + two + last)
        else:
            sides = [across(own, 1), across(own, 2)]
            if step == 1:
                last = [along(cuts_of_first[1])]
            else:
                last = [across(own, 3)]
            steps.append([own] + sides + last)
        if step == 0:
            joined = steps[0][-2:] if group == 4 else []
            cuts_of_first = cut_call(where, steps[0], 2 * own_rows, joined)

    shares = [eval_rows] + [across(eval_rows, k) for k in range(1, group)]
    rows = lax.all_to_all(
        jnp.concatenate(shares, axis=0), ("ring", "core"), split_axis=1, concat_axis=0, tiled=True
    )
    order = chip_at((at_spot - 1 - jnp.arange(ring, dtype=jnp.int32)) % ring)
    order = jnp.concatenate([order * 2 + at_core, order * 2 + 1 - at_core]).astype(jnp.int32)
    where, order = lax.optimization_barrier((where, order))


    factor = inner_rate * depth ** (-0.5)
    terms = []
    piece = back(cuts_of_first[0])
    next_t, next_other_t = turn_call(where, piece)
    chunks = [[0]] + [[step, step + 1] for step in range(1, ring - 1, 2)]
    for chunk in chunks:
        name = chunk[0]
        blocks = [item for step in chunk for item in steps[step]]
        places = places_of(blocks)
        slope = partial = None
        for begin, end in [(0, tiles)]:
            outs = forward_call(
                where, blocks, places, weights, head, hidden_units, own_rows, tile, begin, end,
                partial, slope,
            )
            slope, partial = outs[:2]
            if begin == 0:
                mine_t, other_t = outs[2:]
        partials = [partial] + [across(partial, k) for k in range(1, group)]
        other_t = swap(other_t)
        chunk_pairs = [pairs[step] for step in chunk]
        part_cuts = outer_cuts if name == 0 or chunk is chunks[-1] else [(0, tiles)]
        mine_parts, other_parts = [], []
        for begin, end in part_cuts:
            part = grad_call(chunk_pairs, partials, slope, hidden_units, tile, begin, end)
            mine_parts.append((part, begin))
            other_parts.append((swap(part), begin))
        terms += [(mine_t, mine_parts), (other_t, other_parts)]
        if name == 0:
            next_parts = [(back(part), begin) for part, begin in mine_parts]
    swapped_parts = [(swap(part), begin) for part, begin in next_parts]
    terms += [(next_t, next_parts), (swap(next_other_t), swapped_parts)]

    x_t = join_call([item for item, _ in terms])
    momentum_out = None
    rewards = []
    share = rows.shape[0] // replicas
    for begin, end in outer_cuts:
        part_terms = []
        for _, parts in terms:
            grad, start = [part for part in parts if part[1] <= begin][-1]
            part_terms.append((grad, begin - start))
        momentum_out, near, far = settle_call(
            momentum_out, order, where, x_t, part_terms, momentum, weights, rows, span, factor, replicas,
            tile, begin, end,
        )
        far = swap(far)
        running = near[-share:] + far[-share:]
        for hop in range(1, ring):
            piece = slice((ring - 1 - hop) * share, (ring - hop) * share)
            got = lax.ppermute(
                (near[piece] + far[piece]).astype(bf16),
                "ring",
                [(path[i], path[(i + hop) % ring]) for i in range(ring)],
            )
            running = running + got.astype(f32)
        value = running * depth ** (-0.5)
        rewards.append(
            jnp.sum(value * jax.nn.sigmoid(value) * head[:, begin * tile : end * tile], axis=1)
        )
    partial = sum(rewards)
    each = partial.shape[0] // group
    result = partial[:each]
    for k in range(1, group):
        result = result + across(partial[k * each : (k + 1) * each], k)
    return (momentum_out, result * hidden_units ** (-0.5))


def solution(mesh):
    replicas, group = mesh.shape["replica"], mesh.shape["fsdp"]
    chips = Mesh(mesh.devices.reshape(replicas // 2, 2, group), ("ring", "core", "fsdp"))

    return jax.shard_map(
        shards,
        mesh=chips,
        in_specs=(
            P(None, "fsdp"),
            P("fsdp"),
            P(("ring", "core"), "fsdp"),
            P(None, ("ring", "core", "fsdp"), None),
            P(None, ("ring", "core"), None),
            P(("ring", "core", "fsdp"), None),
        ),
        out_specs=(P(("ring", "core"), "fsdp"), P(("ring", "core", "fsdp"))),
        check_vma=False,
    )
```
